32 devices in a mesh: parts: 2 (over y), wide: 4 (over z), rep: 2 (over x), sub: 2 (over core).
Axes of the slice: x: 2, y: 2, z: 4, core: 2. Of those that a mesh axis runs over, the one named last changes fastest.
Arguments:
- activations: bfloat16 [8, 2048, 512], P(('parts', 'wide'), 'sub'), parts along dimension 0, may hold values from -6 to 6
- deltas: bfloat16 [8, 2048, 512], P(('parts', 'wide'), 'sub'), parts along dimension 0, may hold values from -6 to 6
- act_factor: bfloat16 [512, 512], P(None, 'rep'), as said below
- delta_factor: bfloat16 [512, 512], P(None, 'rep'), as said below
- queries: bfloat16 [1280, 512, 512], P(None, ('rep', 'wide'), 'sub'), may hold values from -0.00059890747 to 0.00059890747
- assignment: int32 [8], P('parts'), parts along dimension 0, may hold values from 0 to 3, each once
- padding: int32 [8], P(('parts', 'wide')), parts along dimension 0, may hold values from 0 to 1023
Outputs:
- scores: float32 [8, 1280], P(('parts', 'wide'), ('rep', 'sub')), parts along dimension 0
The draws below stay inside these ranges and needn't reach their ends.
There are 2 independent parts, one for each index of `parts`. The reference program is written for one: setup_inputs(seed, part) draws one part's arguments, and reference() takes and returns one part's arrays. A program takes and returns all parts, laid end to end along the dimension named above; an argument that names none is the same for every part. Nothing has to cross between parts.
Inputs may be any that keep to these rules, and one draw needn't show every extreme that they name: `act_factor`: symmetric and positive definite. `delta_factor`: symmetric and positive definite. `assignment`: each number once.
All inputs are finite; a program needn't handle non-finite values.
Results may differ from the reference program's by a relative error of at most 0.005.
Values may be sent and summed in bfloat16 or wider, within the bound.
A program may use at most 128 MiB of HBM per device.

```python
import jax
import jax.numpy as jnp
from jax import lax

PROJ = 512
SEQ_LEN = 2048
QUERIES = 1280
SEQS = 4


def make_factor(key):
    first, second = jax.random.split(key)
    diag_part = jnp.exp(jax.random.uniform(first, (PROJ,), jnp.float32, jnp.log(0.5), jnp.log(2.0)))
    noise = jax.random.normal(second, (PROJ, PROJ), jnp.float32)
    symmetric = (noise + noise.T) * (0.2 / (2.0 * PROJ) ** 0.5)
    return (jnp.diag(diag_part) + symmetric).astype(jnp.bfloat16)


def draw_act_factor(key, part):
    return make_factor(jax.random.fold_in(key, 11))


def draw_delta_factor(key, part):
    return make_factor(jax.random.fold_in(key, 23))


def set_ends(values, rng, smallest, high):
    index_at = [jax.random.randint(jax.random.fold_in(rng, axis), (), 0, length) for axis, length in enumerate(values.shape)]
    longest = values.shape.index(max(values.shape))
    next_to = index_at[:longest] + [(index_at[longest] + 1) % values.shape[longest]] + index_at[longest + 1:]
    return values.at[tuple(index_at)].set(smallest).at[tuple(next_to)].set(high)


def with_spikes(entries, key, source, target, parts, factor):
    def block_of(dim):
        return (jnp.arange(entries.shape[dim]) // (entries.shape[dim] // parts)).reshape((-1,) + (1,) * (entries.ndim - 1 - dim))

    one_side = jax.random.permutation(key, parts)[block_of(target)]
    other_side = (block_of(target) + parts // 2) % parts
    return jnp.where((block_of(source) == one_side) | (block_of(source) == other_side), factor * entries, entries)


def level_of(stream_key, extent, shards, smallest, high):
    factor_of = 1.0
    for axis_at, shards_of in shards:
        draws = jax.random.uniform(jax.random.fold_in(jax.random.fold_in(stream_key, 6), axis_at), (shards_of,), jnp.float32, smallest / len(shards), high / len(shards))
        factor_of = factor_of * jnp.repeat(jnp.exp(draws), extent[axis_at] // shards_of).reshape((-1,) + (1,) * (len(extent) - 1 - axis_at))
    return factor_of


def scatter_about(key, extent, deviation, most, cuts=(), kind=jnp.bfloat16):
    result = deviation * jax.random.normal(key, extent, jnp.float32)
    if cuts:
        result = result * level_of(key, extent, cuts, -0.22, 0.18)
    return jnp.clip(result, -most, most).astype(kind)


def heavy_noise(rng, extent, deviation, reach, shards, heavy, dtype=jnp.bfloat16):
    drawn = deviation * jax.random.normal(rng, extent, jnp.float32)
    if shards:
        drawn = drawn * level_of(rng, extent, shards, -0.22, 0.18)
    return jnp.clip(with_spikes(drawn, jax.random.fold_in(rng, 3), *heavy), -reach, reach).astype(dtype)


def setup_inputs(seed: int = 0, part: int = 0) -> dict:
    seeds = jax.random.split(jax.random.key(seed), 8)
    own_keys = jax.random.split(jax.random.fold_in(seeds[7], part), 8)
    return {
        "activations": scatter_about(own_keys[0], (SEQS, SEQ_LEN, PROJ), 1.0, 6.0, ((0, 4), (1, 2))),
        "deltas": scatter_about(own_keys[1], (SEQS, SEQ_LEN, PROJ), 1.0, 6.0, ((0, 4), (1, 2))),
        "act_factor": draw_act_factor(jax.random.fold_in(seeds[7], 71), part),
        "delta_factor": draw_delta_factor(jax.random.fold_in(seeds[7], 71), part),
        "queries": heavy_noise(seeds[4], (QUERIES, PROJ, PROJ), 0.0001, 0.00059890747, ((1, 8), (2, 2)), (1, 0, 8, 2.0)),
        "assignment": jax.random.permutation(own_keys[5], SEQS).astype(jnp.int32),
        "padding": set_ends(jax.random.randint(own_keys[6], (SEQS,), 0, SEQ_LEN // 2), jax.random.fold_in(own_keys[6], 1), 0, (SEQ_LEN // 2) - 1).astype(jnp.int32),
    }


def reference(activations, deltas, act_factor, delta_factor, queries, assignment, padding):
    positions = lax.broadcasted_iota(jnp.int32, (SEQS, SEQ_LEN), 1)
    kept_mask = positions < (SEQ_LEN - padding)[:, None]
    masked = jnp.where(kept_mask[:, :, None], deltas, jnp.zeros((), jnp.bfloat16))
    delta_proj = jnp.dot(masked.reshape(SEQS * SEQ_LEN, PROJ), delta_factor, preferred_element_type=jnp.float32)
    delta_proj = delta_proj.astype(jnp.bfloat16).reshape(SEQS, SEQ_LEN, PROJ)
    act_proj = jnp.dot(activations.reshape(SEQS * SEQ_LEN, PROJ), act_factor, preferred_element_type=jnp.float32)
    act_proj = act_proj.astype(jnp.bfloat16).reshape(SEQS, SEQ_LEN, PROJ)
    grad = jnp.einsum("nti,ntj->nij", delta_proj.astype(jnp.float32), act_proj.astype(jnp.float32))
    grad = grad.astype(jnp.bfloat16)
    raw = jnp.dot(grad.reshape(SEQS, PROJ * PROJ), queries.reshape(QUERIES, PROJ * PROJ).T, preferred_element_type=jnp.float32)
    scores = jnp.zeros((SEQS, QUERIES), jnp.float32).at[assignment].set(raw)
    return scores
```

```python
import functools

import jax
import jax.numpy as jnp
from jax import lax
from jax.experimental import pallas as pl
from jax.experimental.pallas import tpu as pltpu
from jax.sharding import PartitionSpec as P

MESH = pl.DeviceIdType.MESH
UNIT = 32
PIECES = 2


def general_shards(
    activations, deltas, act_factor, delta_factor, queries, assignment, padding
):
    seq_dev, tok_dev, feature_width = activations.shape
    full_length = tok_dev * lax.axis_size("sub")
    token_start = lax.axis_index("sub") * tok_dev
    positions = token_start + lax.broadcasted_iota(jnp.int32, (seq_dev, tok_dev), 1)
    kept_mask = positions < (full_length - padding)[:, None]
    masked = jnp.where(kept_mask[:, :, None], deltas, jnp.zeros((), jnp.bfloat16))
    delta_proj = jnp.einsum(
        "stw,wi->sti", masked, delta_factor, preferred_element_type=jnp.float32
    ).astype(jnp.bfloat16)
    act_proj = jnp.einsum(
        "stw,wj->stj",
        activations,
        lax.all_gather(act_factor, "rep", axis=1, tiled=True),
        preferred_element_type=jnp.float32,
    ).astype(jnp.bfloat16)
    partial_value = jnp.einsum(
        "sti,stj->sij", delta_proj, act_proj, preferred_element_type=jnp.float32
    )
    summed = lax.psum_scatter(partial_value, "sub", scatter_dimension=2, tiled=True).astype(
        jnp.bfloat16
    )
    regrouped = lax.all_to_all(summed, "wide", split_axis=1, concat_axis=0, tiled=True)
    seq_total = regrouped.shape[0]
    grad_rows = regrouped.reshape(seq_total, -1)
    query_rows = queries.reshape(queries.shape[0], -1)
    partial_scores = lax.dot_general(
        grad_rows, query_rows, (((1,), (1,)), ((), ())), preferred_element_type=jnp.float32
    )
    inverse_order = (
        jnp.zeros((seq_total,), jnp.int32)
        .at[assignment]
        .set(jnp.arange(seq_total, dtype=jnp.int32))
    )
    ranked = jnp.take(partial_scores, inverse_order, axis=0)
    by_column = lax.psum_scatter(ranked, ("rep", "sub"), scatter_dimension=1, tiled=True)
    return lax.psum_scatter(by_column, "wide", scatter_dimension=0, tiled=True)


def kernel(
    n_wide,
    pieces,
    assignment_hbm,
    padding_hbm,
    act_hbm,
    delta_hbm,
    act_factor_hbm,
    delta_factor_hbm,
    query_hbm,
    out_ref,
    assignment,
    padding,
    act,
    delta,
    act_factor,
    delta_factor,
    query,
    diag,
    inner_mine,
    inner_theirs,
    factor_cols,
    grad,
    grad_all,
    total_wide,
    total_tall,
    outgoing,
    incoming,
    ready_sem,
    load_sem,
    query_sem,
    diag_sem,
    inner_send_sem,
    inner_recv_sem,
    grad_send_sem,
    grad_recv_sem,
    score_send_sem,
    score_recv_sem,
):
    z = lax.axis_index("wide")
    r = lax.axis_index("rep")
    c = lax.axis_index("sub")
    n_queries, rows, columns = query.shape
    depth = rows // pieces
    block_size = n_queries // 4
    pair = 2 * block_size
    f32, bf16 = jnp.float32, jnp.bfloat16

    def peer(dz, dr, dc):
        return {
            "wide": lax.rem(z + dz, n_wide),
            "rep": lax.rem(r + dr, 2),
            "sub": lax.rem(c + dc, 2),
        }

    def signal_wide(sem, place):
        pl.semaphore_signal(sem, inc=1, device_id={"wide": place}, device_id_type=MESH)

    barrier = pltpu.get_barrier_semaphore()
    for offset in ((0, 0, 1), (0, 1, 0)):
        pl.semaphore_signal(barrier, inc=1, device_id=peer(*offset), device_id_type=MESH)
    has_below, has_above = z > 0, z < n_wide - 1

    @pl.when(has_below)
    def _():
        signal_wide(barrier, z - 1)

    @pl.when(has_above)
    def _():
        signal_wide(barrier, z + 1)

    loads = [
        pltpu.make_async_copy(src, dst, load_sem.at[k])
        for k, (src, dst) in enumerate(
            (
                (padding_hbm, padding),
                (delta_factor_hbm, delta_factor),
                (delta_hbm, delta),
                (act_hbm, act),
                (act_factor_hbm, act_factor),
                (assignment_hbm, assignment),
            )
        )
    ]
    for load in loads:
        load.start()

    def query_copy(piece, block):
        span = pl.ds(pl.multiple_of(block * block_size, block_size), block_size)
        part = pl.ds(piece * depth, depth)
        return pltpu.make_async_copy(
            query_hbm.at[span, part, :], query.at[span, part, :], query_sem.at[piece * 4 + block]
        )

    half = act_factor.shape[1]
    pl.semaphore_wait(barrier, 2 + has_below.astype(jnp.int32) + has_above.astype(jnp.int32))

    @pl.when(has_below & has_above)
    def _():
        signal_wide(ready_sem.at[z + 1], z - 1)
        signal_wide(ready_sem.at[z - 1], z + 1)

    diag_rows = pl.ds(pl.multiple_of(c * half, half), half)
    diag_copy = pltpu.make_async_remote_copy(
        src_ref=act_factor_hbm.at[diag_rows, :],
        dst_ref=diag,
        send_sem=diag_sem.at[0],
        recv_sem=diag_sem.at[1],
        device_id=peer(0, 1, 0),
        device_id_type=MESH,
    )

    @pl.when(r == c)
    def _():
        diag_copy.start()

    for load in loads[:3]:
        load.wait()
    for piece in range(pieces):
        for block in range(4):
            query_copy(piece, block).start()
    tokens = delta.shape[0]
    limit = 2 * tokens - padding[0] - c * tokens
    position = lax.broadcasted_iota(jnp.int32, (tokens, half), 0)
    projected = jnp.dot(delta[...], delta_factor[...], preferred_element_type=f32)
    delta_proj = jnp.where(position < limit, projected, 0.0).astype(bf16)

    loads[3].wait()
    loads[4].wait()
    inner = lax.dot_general(
        delta_proj, act[...], (((0,), (0,)), ((), ())), preferred_element_type=f32
    )
    inner_copies = []
    for s in range(pieces):
        for p in range(n_wide):
            first = p * rows + s * depth
            inner_mine[s, p * depth : (p + 1) * depth, :] = inner[first : first + depth, :]
        copy = pltpu.make_async_remote_copy(
            src_ref=inner_mine.at[s],
            dst_ref=inner_theirs.at[s],
            send_sem=inner_send_sem.at[s],
            recv_sem=inner_recv_sem.at[s],
            device_id=peer(0, 0, 1),
            device_id_type=MESH,
        )
        copy.start()
        inner_copies.append(copy)

    for d in range(2, n_wide):

        @pl.when(z + d < n_wide)
        def _(d=d):
            pl.semaphore_wait(ready_sem.at[z + d], 1)

        @pl.when((z + d < n_wide) & has_below)
        def _(d=d):
            signal_wide(ready_sem.at[z + d], z - 1)

        @pl.when(z - d >= 0)
        def _(d=d):
            pl.semaphore_wait(ready_sem.at[z - d], 1)

        @pl.when((z - d >= 0) & has_above)
        def _(d=d):
            signal_wide(ready_sem.at[z - d], z + 1)

    @pl.when(r == c)
    def _():
        factor_cols[...] = act_factor[...]

    @pl.when(r != c)
    def _():
        mirrored = act_factor[diag_rows, :].astype(f32).T.astype(bf16)
        factor_cols[pl.ds(pl.multiple_of(r * half, half), half), :] = mirrored
        diag_copy.wait_recv()
        factor_cols[diag_rows, :] = diag[...]

    def grad_copy(s, source, place):
        target = pl.ds(pl.multiple_of(place * depth, depth), depth)
        return pltpu.make_async_remote_copy(
            src_ref=grad.at[s, target, :],
            dst_ref=grad_all.at[source, pl.ds(s * depth, depth), :],
            send_sem=grad_send_sem.at[s * n_wide + place],
            recv_sem=grad_recv_sem.at[s * n_wide + source],
            device_id={"wide": place},
            device_id_type=MESH,
        )

    def others():
        for step in range(n_wide - 1):
            low = n_wide - 1 - step
            yield jnp.where(2 * z < n_wide, low - (low <= z), step + (step >= z))

    for s in range(pieces):
        inner_copies[s].wait_recv()
        both = inner_mine[s] + inner_theirs[s]
        high = both.astype(bf16)
        low = (both - high.astype(f32)).astype(bf16)
        gradient = jnp.dot(high, factor_cols[...], preferred_element_type=f32) + jnp.dot(
            low, factor_cols[...], preferred_element_type=f32
        )
        grad[s] = gradient.astype(bf16)
        for place in others():
            grad_copy(s, z, place).start()
        own = pl.ds(pl.multiple_of(z * depth, depth), depth)
        grad_all[z, s * depth : (s + 1) * depth, :] = grad[s, own, :]

    loads[5].wait()
    stack = 8 * n_wide
    place_lane = lax.broadcasted_iota(jnp.int32, (8, stack), 1) // 8
    ranks = jnp.zeros((8, stack), jnp.int32)
    for n in range(n_wide):
        ranks = jnp.where(place_lane == n, assignment[n], ranks)
    rank_rows = lax.broadcasted_iota(jnp.int32, (8, stack), 0)
    places = jnp.where(ranks == rank_rows, 1.0, 0.0).astype(bf16)
    segments = block_size // 16
    gather = jnp.where(
        lax.broadcasted_iota(jnp.int32, (128, block_size), 0) // 8
        == lax.rem(lax.broadcasted_iota(jnp.int32, (128, block_size), 1), 16),
        1.0,
        0.0,
    ).astype(bf16)
    segment_of_lane = lax.broadcasted_iota(jnp.int32, (8, block_size), 1) // 16
    contract = (((1,), (1,)), ((), ()))

    def split(values):
        high = values.astype(bf16)
        return high, (values - high.astype(f32)).astype(bf16)

    def matches(shape, row_axis, lane_axis):
        return lax.rem(lax.broadcasted_iota(jnp.int32, shape, row_axis), 8) == lax.rem(
            lax.broadcasted_iota(jnp.int32, shape, lane_axis), 8
        )

    def weights(a):
        return grad_all[:, 8 * a : 8 * a + 8, :].reshape(stack, columns)

    def tile(start, a):
        span = pl.ds(pl.multiple_of(start, UNIT), UNIT)
        return query[span, 8 * a : 8 * a + 8, :].reshape(8 * UNIT, columns)

    units = block_size // UNIT

    def contractions(s, base):
        wide, tall = [], []
        for first in range(0, units, 2):
            group = range(first, min(units, first + 2))
            got_wide, got_tall = {}, {}
            for a in range(s * depth // 8, (s + 1) * depth // 8):
                for u in group:
                    term = lax.dot_general(
                        weights(a),
                        tile(base + u * UNIT, a),
                        contract,
                        preferred_element_type=f32,
                    )
                    got_wide[u] = got_wide[u] + term if u in got_wide else term
                for u in group:
                    term = lax.dot_general(
                        tile(base + block_size + u * UNIT, a),
                        weights(a),
                        contract,
                        preferred_element_type=f32,
                    )
                    got_tall[u] = got_tall[u] + term if u in got_tall else term
            wide += [got_wide[u] for u in group]
            tall += [got_tall[u] for u in group]
        return wide, tall

    def wait_queries(s, k):
        for block in range(2):
            query_copy(s, 2 * k + block).wait()

    def wait_grads(s):
        for dz in range(1, n_wide):
            grad_copy(s, lax.rem(z + dz, n_wide), z).wait_recv()

    for s in range(pieces - 1):
        wait_grads(s)

        def add_pair(k, carry, s=s):
            wait_queries(s, k)
            wide, tall = contractions(s, k * pair)
            for u in range(units):
                lanes = slice(8 * UNIT * u, 8 * UNIT * (u + 1))
                if s:
                    total_wide[k, :, lanes] += wide[u]
                    total_tall[k, lanes, :] += tall[u]
                else:
                    total_wide[k, :, lanes] = wide[u]
                    total_tall[k, lanes, :] = tall[u]
            return carry

        lax.fori_loop(0, 2, add_pair, 0)

    def device_of(dz, dr, dc):
        where = peer(dz, dr, dc)
        return (where["wide"] * 2 + where["rep"]) * 2 + where["sub"]

    def score_send(k, dz, dc):
        where = {"wide": lax.rem(z + dz, n_wide), "rep": k, "sub": lax.rem(c + dc, 2)}
        return pltpu.make_async_remote_copy(
            src_ref=outgoing.at[k, where["sub"], where["wide"]],
            dst_ref=incoming.at[device_of(0, 0, 0)],
            send_sem=score_send_sem.at[(k * n_wide + dz) * 2 + dc],
            recv_sem=score_recv_sem.at[device_of(0, 0, 0)],
            device_id=where,
            device_id_type=MESH,
        )

    def score_receive(dz, dr, dc):
        slot = device_of(dz, dr, dc)
        return pltpu.make_async_remote_copy(
            src_ref=outgoing.at[0, 0, 0],
            dst_ref=incoming.at[slot],
            send_sem=score_send_sem.at[0],
            recv_sem=score_recv_sem.at[slot],
            device_id=peer(dz, dr, dc),
            device_id_type=MESH,
        )

    final = pieces - 1
    wait_grads(final)

    def score_pair(k, carry):
        wait_queries(final, k)
        wide, tall = contractions(final, k * pair)
        found = []
        for u in range(units):
            lanes = slice(8 * UNIT * u, 8 * UNIT * (u + 1))
            value = wide[u] + total_wide[k, :, lanes] if pieces > 1 else wide[u]
            value = jnp.where(matches(value.shape, 0, 1), value, 0.0)
            high, low = split(value)
            found.append(
                jnp.dot(places, high, preferred_element_type=f32)
                + jnp.dot(places, low, preferred_element_type=f32)
            )
        ranked = jnp.concatenate(found, axis=1)
        stacked = jnp.concatenate(
            [ranked[:, 128 * g : 128 * (g + 1)] for g in range(segments)], axis=0
        )
        high, low = split(stacked)
        spread = jnp.dot(high, gather, preferred_element_type=f32) + jnp.dot(
            low, gather, preferred_element_type=f32
        )
        scores = jnp.zeros((8, block_size), f32)
        for g in range(segments):
            scores = jnp.where(segment_of_lane == g, spread[8 * g : 8 * g + 8], scores)
        for p in range(n_wide):
            outgoing[k, 0, p] = scores[p : p + 1, :]

        sums = []
        for u in range(units):
            lanes = slice(8 * UNIT * u, 8 * UNIT * (u + 1))
            value = tall[u] + total_tall[k, lanes, :] if pieces > 1 else tall[u]
            value = jnp.where(matches(value.shape, 0, 1), value, 0.0)
            sums.append(jnp.sum(value.reshape(UNIT, 8, stack), axis=1))
        high, low = split(jnp.concatenate(sums, axis=0))
        scores = lax.dot_general(
            places, high, contract, preferred_element_type=f32
        ) + lax.dot_general(places, low, contract, preferred_element_type=f32)
        for p in range(n_wide):
            outgoing[k, 1, p] = scores[p : p + 1, :]
        for dz in range(n_wide - 1, 0, -1):
            for dc in (0, 1):
                score_send(k, dz, dc).start()
        score_send(k, 0, 1).start()

        @pl.when(k != r)
        def _():
            score_send(k, 0, 0).start()

        return carry

    lax.fori_loop(0, 2, score_pair, 0)

    @pl.when(r == c)
    def _():
        diag_copy.wait_send()

    for copy in inner_copies:
        copy.wait_send()
    for s in range(pieces):
        for place in others():
            grad_copy(s, z, place).wait_send()
    for k in range(2):
        for dz in range(n_wide):
            for dc in (0, 1):
                if dz or dc:
                    score_send(k, dz, dc).wait_send()

        @pl.when(k != r)
        def _(k=k):
            score_send(k, 0, 0).wait_send()

    result = outgoing[r, c, z]
    for dz in range(n_wide):
        for dr in (0, 1):
            for dc in (0, 1):
                if dz or dr or dc:
                    score_receive(dz, dr, dc).wait_recv()
                    result = result + incoming[device_of(dz, dr, dc)]
    out_ref[...] = result


def fused_shards(
    n_wide, activations, deltas, act_factor, delta_factor, queries, assignment, padding
):
    _, tokens, features = activations.shape
    n_queries, rows, columns = queries.shape
    half = act_factor.shape[1]
    pieces = PIECES
    depth = rows // pieces
    block_size = n_queries // 4
    hbm = pl.BlockSpec(memory_space=pl.ANY)
    dma = pltpu.SemaphoreType.DMA
    bf16, f32 = jnp.bfloat16, jnp.float32
    return pl.pallas_call(
        functools.partial(kernel, n_wide, pieces),
        out_shape=pltpu.VMEM((1, block_size), f32),
        in_specs=[hbm] * 7,
        out_specs=pl.BlockSpec(memory_space=pltpu.VMEM),
        scratch_shapes=[
            pltpu.SMEM((n_wide,), jnp.int32),
            pltpu.SMEM((1,), jnp.int32),
            pltpu.VMEM((tokens, features), bf16),
            pltpu.VMEM((tokens, features), bf16),
            pltpu.VMEM((features, half), bf16),
            pltpu.VMEM((features, half), bf16),
            pltpu.VMEM((n_queries, rows, columns), bf16),
            pltpu.VMEM((half, half), bf16),
            pltpu.VMEM((pieces, n_wide * depth, features), f32),
            pltpu.VMEM((pieces, n_wide * depth, features), f32),
            pltpu.VMEM((features, half), bf16),
            pltpu.VMEM((pieces, n_wide * depth, columns), bf16),
            pltpu.VMEM((n_wide, rows, columns), bf16),
            pltpu.VMEM((2, 8 * n_wide, 8 * block_size), f32),
            pltpu.VMEM((2, 8 * block_size, 8 * n_wide), f32),
            pltpu.VMEM((2, 2, n_wide, 1, block_size), f32),
            pltpu.VMEM((4 * n_wide, 1, block_size), f32),
            pltpu.SemaphoreType.REGULAR((n_wide,)),
            dma((6,)),
            dma((4 * pieces,)),
            dma((2,)),
            dma((pieces,)),
            dma((pieces,)),
            dma((pieces * n_wide,)),
            dma((pieces * n_wide,)),
            dma((4 * n_wide,)),
            dma((4 * n_wide,)),
        ],
        compiler_params=pltpu.CompilerParams(
            collective_id=0, has_side_effects=True, vmem_limit_bytes=60 * 1024 * 1024
        ),
    )(
        assignment,
        padding,
        activations.reshape(tokens, features),
        deltas.reshape(tokens, features),
        act_factor,
        delta_factor,
        queries,
    )


def solution(mesh):
    placed = (
        P(("parts", "wide"), "sub", None),
        P(("parts", "wide"), "sub", None),
        P(None, "rep"),
        P(None, "rep"),
        P(None, ("rep", "wide"), "sub"),
        P("parts"),
        P(("parts", "wide")),
    )
    n_wide, n_rep, n_sub = (mesh.shape[name] for name in ("wide", "rep", "sub"))

    def shards(activations, deltas, act_factor, delta_factor, queries, assignment, padding):
        seq_dev, tokens, features = activations.shape
        n_queries, rows, columns = queries.shape
        fits = (
            seq_dev == 1
            and (n_rep, n_sub) == (2, 2)
            and n_wide <= 8
            and rows % (8 * PIECES) == 0
            and columns % 128 == 0
            and act_factor.shape[1] == columns == n_wide * rows
            and tokens % 16 == 0
            and n_queries % (4 * UNIT) == 0
            and n_queries * rows * columns * 2 <= 44 * 2**20
        )
        run = functools.partial(fused_shards, n_wide) if fits else general_shards
        return run(activations, deltas, act_factor, delta_factor, queries, assignment, padding)

    return jax.shard_map(
        shards,
        mesh=mesh,
        in_specs=placed,
        out_specs=P(("parts", "wide"), ("rep", "sub")),
        check_vma=False,
    )
```

```python
import functools

import jax
import jax.numpy as jnp
from jax import lax
from jax.experimental import pallas as pl
from jax.experimental.pallas import tpu as pltpu
from jax.sharding import PartitionSpec as P

MESH = pl.DeviceIdType.MESH
UNIT = 32
PIECES = 2
EARLY = 1
SPLIT = 6


def general_shards(
    activations, deltas, act_factor, delta_factor, queries, assignment, padding
):
    seq_dev, tok_dev, feature_width = activations.shape
    full_length = tok_dev * lax.axis_size("sub")
    token_start = lax.axis_index("sub") * tok_dev
    positions = token_start + lax.broadcasted_iota(jnp.int32, (seq_dev, tok_dev), 1)
    kept_mask = positions < (full_length - padding)[:, None]
    masked = jnp.where(kept_mask[:, :, None], deltas, jnp.zeros((), jnp.bfloat16))
    delta_proj = jnp.einsum(
        "stw,wi->sti", masked, delta_factor, preferred_element_type=jnp.float32
    ).astype(jnp.bfloat16)
    act_proj = jnp.einsum(
        "stw,wj->stj",
        activations,
        lax.all_gather(act_factor, "rep", axis=1, tiled=True),
        preferred_element_type=jnp.float32,
    ).astype(jnp.bfloat16)
    partial_value = jnp.einsum(
        "sti,stj->sij", delta_proj, act_proj, preferred_element_type=jnp.float32
    )
    summed = lax.psum_scatter(partial_value, "sub", scatter_dimension=2, tiled=True).astype(
        jnp.bfloat16
    )
    regrouped = lax.all_to_all(summed, "wide", split_axis=1, concat_axis=0, tiled=True)
    seq_total = regrouped.shape[0]
    grad_rows = regrouped.reshape(seq_total, -1)
    query_rows = queries.reshape(queries.shape[0], -1)
    partial_scores = lax.dot_general(
        grad_rows, query_rows, (((1,), (1,)), ((), ())), preferred_element_type=jnp.float32
    )
    inverse_order = (
        jnp.zeros((seq_total,), jnp.int32)
        .at[assignment]
        .set(jnp.arange(seq_total, dtype=jnp.int32))
    )
    ranked = jnp.take(partial_scores, inverse_order, axis=0)
    by_column = lax.psum_scatter(ranked, ("rep", "sub"), scatter_dimension=1, tiled=True)
    return lax.psum_scatter(by_column, "wide", scatter_dimension=0, tiled=True)


def kernel(
    n_wide,
    pieces,
    assignment_hbm,
    padding_hbm,
    act_hbm,
    delta_hbm,
    act_factor_hbm,
    delta_factor_hbm,
    query_hbm,
    out_ref,
    assignment,
    padding,
    act,
    delta,
    act_factor,
    delta_factor,
    query,
    diag,
    inner_mine,
    inner_sent,
    inner_theirs,
    factor_near,
    factor_far,
    grad_near,
    grad,
    grad_all,
    total_wide,
    total_tall,
    wide_high,
    wide_low,
    stacked,
    tall_sums,
    outgoing,
    incoming,
    ready_sem,
    load_sem,
    query_sem,
    diag_sem,
    inner_send_sem,
    inner_recv_sem,
    grad_send_sem,
    grad_recv_sem,
    score_send_sem,
    score_recv_sem,
):
    z = lax.axis_index("wide")
    r = lax.axis_index("rep")
    c = lax.axis_index("sub")
    n_queries, rows, columns = query.shape
    depth = rows // pieces
    block_size = n_queries // 4
    pair = 2 * block_size
    f32, bf16 = jnp.float32, jnp.bfloat16

    def peer(dz, dr, dc):
        return {
            "wide": lax.rem(z + dz, n_wide),
            "rep": lax.rem(r + dr, 2),
            "sub": lax.rem(c + dc, 2),
        }

    def signal_wide(sem, place):
        pl.semaphore_signal(sem, inc=1, device_id={"wide": place}, device_id_type=MESH)

    barrier = pltpu.get_barrier_semaphore()
    for offset in ((0, 0, 1), (0, 1, 0)):
        pl.semaphore_signal(barrier, inc=1, device_id=peer(*offset), device_id_type=MESH)
    has_below, has_above = z > 0, z < n_wide - 1

    @pl.when(has_below)
    def _():
        signal_wide(barrier, z - 1)

    @pl.when(has_above)
    def _():
        signal_wide(barrier, z + 1)

    loads = [
        pltpu.make_async_copy(src, dst, load_sem.at[k])
        for k, (src, dst) in enumerate(
            (
                (act_factor_hbm, act_factor),
                (padding_hbm, padding),
                (delta_factor_hbm, delta_factor),
                (delta_hbm, delta),
                (act_hbm, act),
                (assignment_hbm, assignment),
            )
        )
    ]
    for load in loads:
        load.start()

    units = block_size // UNIT
    tiles = rows // 8
    stages = tuple((0, 0, units, s * tiles // pieces, (s + 1) * tiles // pieces) for s in range(pieces))
    stages += ((1, 0, SPLIT, 0, tiles), (1, SPLIT, units, 0, tiles))

    def query_copies(stage):
        k, low, high, top, bottom = stages[stage]
        for side in (0, 1):
            first = k * pair + side * block_size + low * UNIT
            span = pl.ds(first, (high - low) * UNIT)
            part = pl.ds(8 * top, 8 * (bottom - top))
            yield pltpu.make_async_copy(
                query_hbm.at[span, part, :], query.at[span, part, :], query_sem.at[2 * stage + side]
            )

    query_starts = [copy for stage in range(len(stages)) for copy in query_copies(stage)]
    for copy in query_starts[:EARLY]:
        copy.start()

    half = act_factor.shape[1]
    pl.semaphore_wait(barrier, 2 + has_below.astype(jnp.int32) + has_above.astype(jnp.int32))

    @pl.when(has_below & has_above)
    def _():
        signal_wide(ready_sem.at[z + 1], z - 1)
        signal_wide(ready_sem.at[z - 1], z + 1)

    quarter = half // 2
    diag_copies = []
    for k, width in enumerate((quarter, half)):
        rows_at = pl.ds(pl.multiple_of(c * half + k * quarter, quarter), quarter)
        diag_copies.append(
            pltpu.make_async_remote_copy(
                src_ref=act_factor.at[rows_at, pl.ds(0, width)],
                dst_ref=diag.at[pl.ds(k * quarter, quarter), pl.ds(0, width)],
                send_sem=diag_sem.at[2 * k],
                recv_sem=diag_sem.at[2 * k + 1],
                device_id=peer(0, 1, 0),
                device_id_type=MESH,
            )
        )

    loads[0].wait()

    @pl.when(r == c)
    def _():
        for copy in diag_copies:
            copy.start()

    for load in loads[1:4]:
        load.wait()
    tokens = delta.shape[0]
    limit = 2 * tokens - padding[0] - c * tokens
    position = lax.broadcasted_iota(jnp.int32, (tokens, half), 0)
    projected = jnp.dot(delta[...], delta_factor[...], preferred_element_type=f32)
    delta_proj = jnp.where(position < limit, projected, 0.0).astype(bf16)

    loads[4].wait()
    for copy in query_starts[EARLY:]:
        copy.start()
    inner = lax.dot_general(
        delta_proj, act[...], (((0,), (0,)), ((), ())), preferred_element_type=f32
    )
    inner_copies = []
    for s in range(pieces):
        for p in range(n_wide):
            first = p * rows + s * depth
            part = inner[first : first + depth, :]
            inner_sent[s, p * depth : (p + 1) * depth, :] = part.astype(bf16)
            inner_mine[s, p * depth : (p + 1) * depth, :] = part
        copy = pltpu.make_async_remote_copy(
            src_ref=inner_sent.at[s],
            dst_ref=inner_theirs.at[s],
            send_sem=inner_send_sem.at[s],
            recv_sem=inner_recv_sem.at[s],
            device_id=peer(0, 0, 1),
            device_id_type=MESH,
        )
        copy.start()
        inner_copies.append(copy)

    for d in range(2, n_wide):

        @pl.when(z + d < n_wide)
        def _(d=d):
            pl.semaphore_wait(ready_sem.at[z + d], 1)

        @pl.when((z + d < n_wide) & has_below)
        def _(d=d):
            signal_wide(ready_sem.at[z + d], z - 1)

        @pl.when(z - d >= 0)
        def _(d=d):
            pl.semaphore_wait(ready_sem.at[z - d], 1)

        @pl.when((z - d >= 0) & has_above)
        def _(d=d):
            signal_wide(ready_sem.at[z - d], z + 1)

    near = pl.ds(pl.multiple_of(r * half, half), half)
    far = pl.ds(pl.multiple_of((1 - r) * half, half), half)

    @pl.when(r == c)
    def _():
        factor_near[...] = act_factor[near, :]

    @pl.when(r != c)
    def _():
        factor_near[...] = act_factor[far, :].astype(f32).T.astype(bf16)

    def grad_copy(s, source, place):
        target = pl.ds(pl.multiple_of(place * depth, depth), depth)
        return pltpu.make_async_remote_copy(
            src_ref=grad.at[s, target, :],
            dst_ref=grad_all.at[source, pl.ds(s * depth, depth), :],
            send_sem=grad_send_sem.at[s],
            recv_sem=grad_recv_sem.at[s],
            device_id={"wide": place},
            device_id_type=MESH,
        )

    def others():
        for step in range(n_wide - 1):
            low = n_wide - 1 - step
            yield jnp.where(2 * z < n_wide, low - (low <= z), step + (step >= z))

    def product(s, lanes, factor):
        both = inner_mine[s, :, lanes] + inner_theirs[s, :, lanes].astype(f32)
        high = both.astype(bf16)
        low = (both - high.astype(f32)).astype(bf16)
        return jnp.dot(high, factor[...], preferred_element_type=f32) + jnp.dot(
            low, factor[...], preferred_element_type=f32
        )

    for s in range(pieces):
        inner_copies[s].wait_recv()
        grad_near[s] = product(s, near, factor_near)

    @pl.when(r == c)
    def _():
        factor_far[...] = act_factor[far, :]

    @pl.when(r != c)
    def _():
        for copy in diag_copies:
            copy.wait_recv()
        factor_far[:, :quarter] = diag[:, :quarter]
        factor_far[quarter:, quarter:] = diag[quarter:, quarter:]
        factor_far[:quarter, quarter:] = diag[quarter:, :quarter].astype(f32).T.astype(bf16)

    for s in range(pieces):
        grad[s] = (grad_near[s] + product(s, far, factor_far)).astype(bf16)
        for place in others():
            grad_copy(s, z, place).start()
        own = pl.ds(pl.multiple_of(z * depth, depth), depth)
        grad_all[z, s * depth : (s + 1) * depth, :] = grad[s, own, :]

    loads[5].wait()
    stack = 8 * n_wide
    place_lane = lax.broadcasted_iota(jnp.int32, (8, stack), 1) // 8
    ranks = jnp.zeros((8, stack), jnp.int32)
    for n in range(n_wide):
        ranks = jnp.where(place_lane == n, assignment[n], ranks)
    rank_rows = lax.broadcasted_iota(jnp.int32, (8, stack), 0)
    places = jnp.where(ranks == rank_rows, 1.0, 0.0).astype(bf16)
    segments = block_size // 16
    gather = jnp.where(
        lax.broadcasted_iota(jnp.int32, (128, block_size), 0) // 8
        == lax.rem(lax.broadcasted_iota(jnp.int32, (128, block_size), 1), 16),
        1.0,
        0.0,
    ).astype(bf16)
    segment_of_lane = lax.broadcasted_iota(jnp.int32, (8, block_size), 1) // 16
    contract = (((1,), (1,)), ((), ()))

    def split(values):
        high = values.astype(bf16)
        return high, (values - high.astype(f32)).astype(bf16)

    def matches(shape, row_axis, lane_axis):
        return lax.rem(lax.broadcasted_iota(jnp.int32, shape, row_axis), 8) == lax.rem(
            lax.broadcasted_iota(jnp.int32, shape, lane_axis), 8
        )

    def weights(a):
        return grad_all[:, 8 * a : 8 * a + 8, :].reshape(stack, columns)

    def tile(start, a):
        span = pl.ds(pl.multiple_of(start, UNIT), UNIT)
        return query[span, 8 * a : 8 * a + 8, :].reshape(8 * UNIT, columns)

    def device_of(place):
        return (place["wide"] * 2 + place["rep"]) * 2 + place["sub"]

    slot = device_of(peer(0, 0, 0))

    def score_send(k, where):
        return pltpu.make_async_remote_copy(
            src_ref=outgoing.at[k, where["sub"], where["wide"]],
            dst_ref=incoming.at[slot],
            send_sem=score_send_sem,
            recv_sem=score_recv_sem,
            device_id=where,
            device_id_type=MESH,
        )

    def send_side(k, side):
        for dz in range(n_wide - 1, 0, -1):
            where = {"wide": lax.rem(z + dz, n_wide), "rep": k, "sub": side}
            score_send(k, where).start()

    def send_sibling(k):
        score_send(k, {"wide": z, "rep": k, "sub": 1 - c}).start()

    def lanes_of(u):
        return slice(8 * UNIT * u, 8 * UNIT * (u + 1))

    def rank_wide(k, chosen):
        for u in chosen:
            ranked = jnp.dot(places, wide_high[k, :, lanes_of(u)], preferred_element_type=f32)
            ranked += jnp.dot(places, wide_low[k, :, lanes_of(u)], preferred_element_type=f32)
            for g in range(UNIT // 16):
                stacked[k, u * (UNIT // 16) + g] = ranked[:, 128 * g : 128 * (g + 1)]

    def finish_wide(k):
        high, low = split(stacked[k].reshape(8 * segments, 128))
        spread = jnp.dot(high, gather, preferred_element_type=f32) + jnp.dot(
            low, gather, preferred_element_type=f32
        )
        scores = jnp.zeros((8, block_size), f32)
        for g in range(segments):
            scores = jnp.where(segment_of_lane == g, spread[8 * g : 8 * g + 8], scores)
        for p in range(n_wide):
            outgoing[k, 0, p] = scores[p : p + 1, :]
        send_side(k, 0)

    def finish_tall(k):
        high, low = split(tall_sums[k])
        scores = lax.dot_general(
            places, high, contract, preferred_element_type=f32
        ) + lax.dot_general(places, low, contract, preferred_element_type=f32)
        for p in range(n_wide):
            outgoing[k, 1, p] = scores[p : p + 1, :]
        send_side(k, 1)

    def score_stage(stage, tasks):
        for copy in query_copies(stage):
            copy.wait()
        k, low, high, top, bottom = stages[stage]
        base = k * pair
        for first in range(low, high, 2):
            group = range(first, min(high, first + 2))
            wide, tall = {}, {}
            for a in range(top, bottom):
                for u in group:
                    term = lax.dot_general(
                        weights(a), tile(base + u * UNIT, a), contract, preferred_element_type=f32
                    )
                    wide[u] = wide[u] + term if u in wide else term
                for u in group:
                    term = lax.dot_general(
                        tile(base + block_size + u * UNIT, a),
                        weights(a),
                        contract,
                        preferred_element_type=f32,
                    )
                    tall[u] = tall[u] + term if u in tall else term
            for u in group:
                if top:
                    wide[u] += total_wide[:, lanes_of(u)]
                    tall[u] += total_tall[lanes_of(u), :]
                if bottom < tiles:
                    total_wide[:, lanes_of(u)] = wide[u]
                    total_tall[lanes_of(u), :] = tall[u]
                    continue
                value = jnp.where(matches(wide[u].shape, 0, 1), wide[u], 0.0)
                wide_high[k, :, lanes_of(u)], wide_low[k, :, lanes_of(u)] = split(value)
                value = jnp.where(matches(tall[u].shape, 0, 1), tall[u], 0.0)
                tall_sums[k, UNIT * u : UNIT * (u + 1), :] = jnp.sum(
                    value.reshape(UNIT, 8, stack), axis=1
                )
            if tasks:
                tasks.pop(0)()

    def wait_grads(s):
        grads = grad.at[s, pl.ds(0, (n_wide - 1) * depth), :]
        pltpu.make_async_copy(grads, grads, grad_recv_sem.at[s]).wait()

    def first_task():
        rank_wide(0, range(units))
        finish_tall(0)

    def second_task():
        finish_wide(0)
        send_sibling(0)

    for s in range(pieces):
        wait_grads(s)
        score_stage(s, [])
    score_stage(pieces, [first_task, second_task])
    rep_copy = score_send(1 - r, peer(0, 1, 0))

    @pl.when(r == 1)
    def _():
        rep_copy.start()

    score_stage(pieces + 1, [lambda: rank_wide(1, range(SPLIT))])
    rank_wide(1, range(SPLIT, units))
    finish_tall(1)
    finish_wide(1)
    send_sibling(1)

    @pl.when(r == 0)
    def _():
        rep_copy.start()


    incoming[slot] = outgoing[r, c, z]

    @pl.when(r == c)
    def _():
        for copy in diag_copies:
            copy.wait_send()

    for copy in inner_copies:
        copy.wait_send()
    for s in range(pieces):
        grads = grad.at[s, pl.ds(0, (n_wide - 1) * depth), :]
        pltpu.make_async_copy(grads, grads, grad_send_sem.at[s]).wait()
    messages = incoming.at[pl.ds(0, 4 * n_wide - 1)]
    pltpu.make_async_copy(messages, messages, score_recv_sem).wait()
    pltpu.make_async_copy(messages, messages, score_send_sem).wait()
    out_ref[...] = jnp.sum(incoming[...], axis=0)


def fused_shards(
    n_wide, activations, deltas, act_factor, delta_factor, queries, assignment, padding
):
    _, tokens, features = activations.shape
    n_queries, rows, columns = queries.shape
    half = act_factor.shape[1]
    pieces = PIECES
    depth = rows // pieces
    block_size = n_queries // 4
    hbm = pl.BlockSpec(memory_space=pl.ANY)
    dma = pltpu.SemaphoreType.DMA
    bf16, f32 = jnp.bfloat16, jnp.float32
    return pl.pallas_call(
        functools.partial(kernel, n_wide, pieces),
        out_shape=pltpu.VMEM((1, block_size), f32),
        in_specs=[hbm] * 7,
        out_specs=pl.BlockSpec(memory_space=pltpu.VMEM),
        scratch_shapes=[
            pltpu.SMEM((n_wide,), jnp.int32),
            pltpu.SMEM((1,), jnp.int32),
            pltpu.VMEM((tokens, features), bf16),
            pltpu.VMEM((tokens, features), bf16),
            pltpu.VMEM((features, half), bf16),
            pltpu.VMEM((features, half), bf16),
            pltpu.VMEM((n_queries, rows, columns), bf16),
            pltpu.VMEM((half, half), bf16),
            pltpu.VMEM((pieces, n_wide * depth, features), f32),
            pltpu.VMEM((pieces, n_wide * depth, features), bf16),
            pltpu.VMEM((pieces, n_wide * depth, features), bf16),
            pltpu.VMEM((half, half), bf16),
            pltpu.VMEM((half, half), bf16),
            pltpu.VMEM((pieces, n_wide * depth, columns), f32),
            pltpu.VMEM((pieces, n_wide * depth, columns), bf16),
            pltpu.VMEM((n_wide, rows, columns), bf16),
            pltpu.VMEM((8 * n_wide, 8 * block_size), f32),
            pltpu.VMEM((8 * block_size, 8 * n_wide), f32),
            pltpu.VMEM((2, 8 * n_wide, 8 * block_size), bf16),
            pltpu.VMEM((2, 8 * n_wide, 8 * block_size), bf16),
            pltpu.VMEM((2, block_size // 16, 8, 128), f32),
            pltpu.VMEM((2, block_size, 8 * n_wide), f32),
            pltpu.VMEM((2, 2, n_wide, 1, block_size), f32),
            pltpu.VMEM((4 * n_wide, 1, block_size), f32),
            pltpu.SemaphoreType.REGULAR((n_wide,)),
            dma((6,)),
            dma((2 * pieces + 4,)),
            dma((4,)),
            dma((pieces,)),
            dma((pieces,)),
            dma((pieces,)),
            dma((pieces,)),
            dma,
            dma,
        ],
        compiler_params=pltpu.CompilerParams(
            collective_id=0, has_side_effects=True, vmem_limit_bytes=60 * 1024 * 1024
        ),
    )(
        assignment,
        padding,
        activations.reshape(tokens, features),
        deltas.reshape(tokens, features),
        act_factor,
        delta_factor,
        queries,
    )


def solution(mesh):
    placed = (
        P(("parts", "wide"), "sub", None),
        P(("parts", "wide"), "sub", None),
        P(None, "rep"),
        P(None, "rep"),
        P(None, ("rep", "wide"), "sub"),
        P("parts"),
        P(("parts", "wide")),
    )
    n_wide, n_rep, n_sub = (mesh.shape[name] for name in ("wide", "rep", "sub"))

    def shards(activations, deltas, act_factor, delta_factor, queries, assignment, padding):
        seq_dev, tokens, features = activations.shape
        n_queries, rows, columns = queries.shape
        fits = (
            seq_dev == 1
            and (n_rep, n_sub) == (2, 2)
            and n_wide <= 8
            and rows % (8 * PIECES) == 0
            and columns % 128 == 0
            and act_factor.shape[1] == columns == n_wide * rows
            and tokens % 16 == 0
            and n_queries % (4 * UNIT) == 0
            and n_queries * rows * columns * 2 <= 44 * 2**20
        )
        run = functools.partial(fused_shards, n_wide) if fits else general_shards
        return run(activations, deltas, act_factor, delta_factor, queries, assignment, padding)

    return jax.shard_map(
        shards,
        mesh=mesh,
        in_specs=placed,
        out_specs=P(("parts", "wide"), ("rep", "sub")),
        check_vma=False,
    )
```

```python
import functools

import jax
import jax.numpy as jnp
from jax import lax
from jax.experimental import pallas as pl
from jax.experimental.pallas import tpu as pltpu
from jax.sharding import PartitionSpec as P

MESH = pl.DeviceIdType.MESH
UNIT = 32
PIECES = 2
EARLY = 2
SPLIT = 6
DIAG_PARTS = 1
LEAD = 4


def general_shards(
    activations, deltas, act_factor, delta_factor, queries, assignment, padding
):
    seq_dev, tok_dev, feature_width = activations.shape
    full_length = tok_dev * lax.axis_size("sub")
    token_start = lax.axis_index("sub") * tok_dev
    positions = token_start + lax.broadcasted_iota(jnp.int32, (seq_dev, tok_dev), 1)
    kept_mask = positions < (full_length - padding)[:, None]
    masked = jnp.where(kept_mask[:, :, None], deltas, jnp.zeros((), jnp.bfloat16))
    delta_proj = jnp.einsum(
        "stw,wi->sti", masked, delta_factor, preferred_element_type=jnp.float32
    ).astype(jnp.bfloat16)
    act_proj = jnp.einsum(
        "stw,wj->stj",
        activations,
        lax.all_gather(act_factor, "rep", axis=1, tiled=True),
        preferred_element_type=jnp.float32,
    ).astype(jnp.bfloat16)
    partial_value = jnp.einsum(
        "sti,stj->sij", delta_proj, act_proj, preferred_element_type=jnp.float32
    )
    summed = lax.psum_scatter(partial_value, "sub", scatter_dimension=2, tiled=True).astype(
        jnp.bfloat16
    )
    regrouped = lax.all_to_all(summed, "wide", split_axis=1, concat_axis=0, tiled=True)
    seq_total = regrouped.shape[0]
    grad_rows = regrouped.reshape(seq_total, -1)
    query_rows = queries.reshape(queries.shape[0], -1)
    partial_scores = lax.dot_general(
        grad_rows, query_rows, (((1,), (1,)), ((), ())), preferred_element_type=jnp.float32
    )
    inverse_order = (
        jnp.zeros((seq_total,), jnp.int32)
        .at[assignment]
        .set(jnp.arange(seq_total, dtype=jnp.int32))
    )
    ranked = jnp.take(partial_scores, inverse_order, axis=0)
    by_column = lax.psum_scatter(ranked, ("rep", "sub"), scatter_dimension=1, tiled=True)
    return lax.psum_scatter(by_column, "wide", scatter_dimension=0, tiled=True)


def kernel(
    n_wide,
    pieces,
    assignment_hbm,
    padding_hbm,
    act_hbm,
    delta_hbm,
    act_factor_hbm,
    delta_factor_hbm,
    query_hbm,
    out_ref,
    assignment,
    padding,
    act,
    delta,
    act_factor,
    delta_factor,
    query,
    diag,
    inner_mine,
    inner_sent,
    inner_theirs,
    factor_near,
    factor_far,
    grad_near,
    grad,
    grad_all,
    total_wide,
    stacked,
    tall_sums,
    outgoing,
    incoming,
    ready_sem,
    load_sem,
    query_sem,
    diag_sem,
    inner_send_sem,
    inner_recv_sem,
    grad_send_sem,
    grad_recv_sem,
    score_send_sem,
    score_recv_sem,
):
    z = lax.axis_index("wide")
    r = lax.axis_index("rep")
    c = lax.axis_index("sub")
    n_queries, rows, columns = query.shape
    depth = rows // pieces
    block_size = n_queries // 4
    pair = 2 * block_size
    f32, bf16 = jnp.float32, jnp.bfloat16

    def peer(dz, dr, dc):
        return {
            "wide": lax.rem(z + dz, n_wide),
            "rep": lax.rem(r + dr, 2),
            "sub": lax.rem(c + dc, 2),
        }

    def signal_wide(sem, place):
        pl.semaphore_signal(sem, inc=1, device_id={"wide": place}, device_id_type=MESH)

    barrier = pltpu.get_barrier_semaphore()
    for offset in ((0, 0, 1), (0, 1, 0)):
        pl.semaphore_signal(barrier, inc=1, device_id=peer(*offset), device_id_type=MESH)
    has_below, has_above = z > 0, z < n_wide - 1

    @pl.when(has_below)
    def _():
        signal_wide(barrier, z - 1)

    @pl.when(has_above)
    def _():
        signal_wide(barrier, z + 1)

    loads = [
        pltpu.make_async_copy(src, dst, load_sem.at[k])
        for k, (src, dst) in enumerate(
            (
                (act_factor_hbm, act_factor),
                (padding_hbm, padding),
                (delta_factor_hbm, delta_factor),
                (delta_hbm, delta),
                (act_hbm, act),
                (assignment_hbm, assignment),
            )
        )
    ]
    for load in loads:
        load.start()

    units = block_size // UNIT
    tiles = rows // 8
    cut = tiles // pieces
    stages = (
        ((0, 0, LEAD, 0, cut),),
        ((0, 0, LEAD, cut, tiles), (0, LEAD, units, 0, tiles)),
        ((1, 0, SPLIT, 0, tiles),),
        ((1, SPLIT, units, 0, tiles),),
    )
    query_slots = [(stage, part) for stage in stages for part in stage]

    def query_copies(stage):
        for part in stages[stage]:
            k, low, high, top, bottom = part
            place = query_slots.index((stages[stage], part))
            for side in (0, 1):
                first = k * pair + side * block_size + low * UNIT
                span = pl.ds(first, (high - low) * UNIT)
                lines = pl.ds(8 * top, 8 * (bottom - top))
                yield pltpu.make_async_copy(
                    query_hbm.at[span, lines, :],
                    query.at[span, lines, :],
                    query_sem.at[2 * place + side],
                )

    query_starts = [copy for stage in range(len(stages)) for copy in query_copies(stage)]
    for copy in query_starts[:EARLY]:
        copy.start()

    half = act_factor.shape[1]
    pl.semaphore_wait(barrier, 2 + has_below.astype(jnp.int32) + has_above.astype(jnp.int32))

    @pl.when(has_below & has_above)
    def _():
        signal_wide(ready_sem.at[z + 1], z - 1)
        signal_wide(ready_sem.at[z - 1], z + 1)

    quarter = half // 2
    piece_rows = quarter // DIAG_PARTS

    def diag_copy(k):
        width = quarter if k < DIAG_PARTS else half
        return pltpu.make_async_remote_copy(
            src_ref=act_factor.at[
                pl.ds(pl.multiple_of(c * half + k * piece_rows, piece_rows), piece_rows),
                pl.ds(0, width),
            ],
            dst_ref=diag.at[pl.ds(k * piece_rows, piece_rows), pl.ds(0, width)],
            send_sem=diag_sem.at[0],
            recv_sem=diag_sem.at[1],
            device_id=peer(0, 1, 0),
            device_id_type=MESH,
        )

    diag_bytes = diag.at[pl.ds(0, quarter + quarter // 2), :]

    loads[0].wait()

    @pl.when(r == c)
    def _():
        for k in range(2 * DIAG_PARTS):
            diag_copy(k).start()

    for load in loads[1:4]:
        load.wait()
    tokens = delta.shape[0]
    limit = 2 * tokens - padding[0] - c * tokens
    position = lax.broadcasted_iota(jnp.int32, (tokens, half), 0)
    projected = jnp.dot(delta[...], delta_factor[...], preferred_element_type=f32)
    delta_proj = jnp.where(position < limit, projected, 0.0).astype(bf16)

    loads[4].wait()
    for copy in query_starts[EARLY:]:
        copy.start()
    inner = lax.dot_general(
        delta_proj, act[...], (((0,), (0,)), ((), ())), preferred_element_type=f32
    )
    inner_copies = []
    for s in range(pieces):
        for p in range(n_wide):
            first = p * rows + s * depth
            part = inner[first : first + depth, :]
            inner_sent[s, p * depth : (p + 1) * depth, :] = part.astype(bf16)
            inner_mine[s, p * depth : (p + 1) * depth, :] = part
        copy = pltpu.make_async_remote_copy(
            src_ref=inner_sent.at[s],
            dst_ref=inner_theirs.at[s],
            send_sem=inner_send_sem.at[s],
            recv_sem=inner_recv_sem.at[s],
            device_id=peer(0, 0, 1),
            device_id_type=MESH,
        )
        copy.start()
        inner_copies.append(copy)

    stacked[...] = jnp.zeros(stacked.shape, f32)

    for d in range(2, n_wide):

        @pl.when((z + d < n_wide) & has_below)
        def _(d=d):
            pl.semaphore_wait(ready_sem.at[z + d], 1)
            signal_wide(ready_sem.at[z + d], z - 1)

        @pl.when((z - d >= 0) & has_above)
        def _(d=d):
            pl.semaphore_wait(ready_sem.at[z - d], 1)
            signal_wide(ready_sem.at[z - d], z + 1)

    near = pl.ds(pl.multiple_of(r * half, half), half)
    far = pl.ds(pl.multiple_of((1 - r) * half, half), half)

    @pl.when(r == c)
    def _():
        factor_near[...] = act_factor[near, :]
        factor_far[...] = act_factor[far, :]

    @pl.when(r != c)
    def _():
        factor_near[...] = act_factor[far, :].astype(f32).T.astype(bf16)

    def grad_copy(s, source, place):
        target = pl.ds(pl.multiple_of(place * depth, depth), depth)
        return pltpu.make_async_remote_copy(
            src_ref=grad.at[s, target, :],
            dst_ref=grad_all.at[source, pl.ds(s * depth, depth), :],
            send_sem=grad_send_sem.at[s],
            recv_sem=grad_recv_sem.at[s],
            device_id={"wide": place},
            device_id_type=MESH,
        )

    def others():
        for step in range(n_wide - 1):
            low = n_wide - 1 - step
            yield jnp.where(2 * z < n_wide, low - (low <= z), step + (step >= z))

    def product(s, lanes, factor):
        both = inner_mine[s, :, lanes] + inner_theirs[s, :, lanes].astype(f32)
        high = both.astype(bf16)
        low = (both - high.astype(f32)).astype(bf16)
        return jnp.dot(high, factor[...], preferred_element_type=f32) + jnp.dot(
            low, factor[...], preferred_element_type=f32
        )

    def wait_ends():
        @pl.when(z == 0)
        def _():
            for place in range(2, n_wide):
                pl.semaphore_wait(ready_sem.at[place], 1)

        @pl.when(z == n_wide - 1)
        def _():
            for place in range(n_wide - 2):
                pl.semaphore_wait(ready_sem.at[place], 1)

    inner_copies[0].wait_recv()
    grad_near[...] = product(0, near, factor_near)

    @pl.when(r != c)
    def _():
        pltpu.make_async_copy(diag_bytes, diag_bytes, diag_sem.at[1]).wait()
        factor_far[:, :quarter] = diag[:, :quarter]
        factor_far[quarter:, quarter:] = diag[quarter:, quarter:]
        factor_far[:quarter, quarter:] = diag[quarter:, :quarter].astype(f32).T.astype(bf16)

    for s in range(pieces):
        if s:
            inner_copies[s].wait_recv()
            grad_near[...] = product(s, near, factor_near)
        grad[s] = (grad_near[...] + product(s, far, factor_far)).astype(bf16)
        if s == 0:
            wait_ends()
        for place in others():
            grad_copy(s, z, place).start()
        own = pl.ds(pl.multiple_of(z * depth, depth), depth)
        grad_all[z, s * depth : (s + 1) * depth, :] = grad[s, own, :]

    loads[5].wait()
    stack = 8 * n_wide
    place_lane = lax.broadcasted_iota(jnp.int32, (8, stack), 1) // 8
    ranks = jnp.zeros((8, stack), jnp.int32)
    for n in range(n_wide):
        ranks = jnp.where(place_lane == n, assignment[n], ranks)
    rank_rows = lax.broadcasted_iota(jnp.int32, (8, stack), 0)
    places = jnp.where(ranks == rank_rows, 1.0, 0.0).astype(bf16)
    segments = block_size // 16
    gather = jnp.where(
        lax.broadcasted_iota(jnp.int32, (128, block_size), 0) // 8
        == lax.rem(lax.broadcasted_iota(jnp.int32, (128, block_size), 1), 16),
        1.0,
        0.0,
    ).astype(bf16)
    segment_of_lane = lax.broadcasted_iota(jnp.int32, (8, block_size), 1) // 16
    contract = (((1,), (1,)), ((), ()))

    def split(values):
        high = values.astype(bf16)
        return high, (values - high.astype(f32)).astype(bf16)

    def matches(shape, row_axis, lane_axis):
        return lax.rem(lax.broadcasted_iota(jnp.int32, shape, row_axis), 8) == lax.rem(
            lax.broadcasted_iota(jnp.int32, shape, lane_axis), 8
        )

    def weights(a):
        return grad_all[:, 8 * a : 8 * a + 8, :].reshape(stack, columns)

    def tile(start, a):
        span = pl.ds(pl.multiple_of(start, UNIT), UNIT)
        return query[span, 8 * a : 8 * a + 8, :].reshape(8 * UNIT, columns)

    def device_of(place):
        return (place["wide"] * 2 + place["rep"]) * 2 + place["sub"]

    slot = device_of(peer(0, 0, 0))

    def score_send(k, where):
        return pltpu.make_async_remote_copy(
            src_ref=outgoing.at[k, where["sub"], where["wide"]],
            dst_ref=incoming.at[slot],
            send_sem=score_send_sem,
            recv_sem=score_recv_sem,
            device_id=where,
            device_id_type=MESH,
        )

    def send_side(k, side):
        for dz in range(n_wide - 1, 0, -1):
            where = {"wide": lax.rem(z + dz, n_wide), "rep": k, "sub": side}
            score_send(k, where).start()

    def send_sibling(k):
        score_send(k, {"wide": z, "rep": k, "sub": 1 - c}).start()

    def lanes_of(u):
        return slice(8 * UNIT * u, 8 * UNIT * (u + 1))

    def finish_wide(k):
        high, low = split(stacked[k].reshape(8 * segments, 128))
        spread = jnp.dot(high, gather, preferred_element_type=f32) + jnp.dot(
            low, gather, preferred_element_type=f32
        )
        scores = jnp.zeros((8, block_size), f32)
        for g in range(segments):
            scores = jnp.where(segment_of_lane == g, spread[8 * g : 8 * g + 8], scores)
        for p in range(n_wide):
            row = scores[0:1, :]
            for n in range(1, n_wide):
                row = jnp.where(assignment[n] == p, scores[n : n + 1, :], row)
            outgoing[k, 0, p] = row
        send_side(k, 0)

    def finish_tall(k):
        high, low = split(tall_sums[k])
        scores = lax.dot_general(
            places, high, contract, preferred_element_type=f32
        ) + lax.dot_general(places, low, contract, preferred_element_type=f32)
        for p in range(n_wide):
            outgoing[k, 1, p] = scores[p : p + 1, :]
        send_side(k, 1)

    def score_stage(stage, tasks):
        for copy in query_copies(stage):
            copy.wait()
        groups = [
            (part, first) for part in stages[stage] for first in range(part[1], part[2], 2)
        ]
        for (k, low, high, top, bottom), first in groups:
            base = k * pair
            group = range(first, min(high, first + 2))
            wide, tall = {}, {}
            for a in range(top, bottom):
                for u in group:
                    term = lax.dot_general(
                        weights(a), tile(base + u * UNIT, a), contract, preferred_element_type=f32
                    )
                    wide[u] = wide[u] + term if u in wide else term
                for u in group:
                    term = lax.dot_general(
                        tile(base + block_size + u * UNIT, a),
                        weights(a),
                        contract,
                        preferred_element_type=f32,
                    )
                    tall[u] = tall[u] + term if u in tall else term
            for u in group:
                span = slice(UNIT * u, UNIT * (u + 1))
                value = jnp.where(matches(tall[u].shape, 0, 1), tall[u], 0.0)
                summed = jnp.sum(value.reshape(UNIT, 8, stack), axis=1)
                tall_sums[k, span, :] = tall_sums[k, span, :] + summed if top else summed
                value = jnp.where(matches(wide[u].shape, 0, 1), wide[u], 0.0)
                if top:
                    value = value + total_wide[:, lanes_of(u)]
                if bottom < tiles:
                    total_wide[:, lanes_of(u)] = value
                    continue
                value = jnp.sum(value.reshape(n_wide, 8, 8 * UNIT), axis=1)
                for g in range(UNIT // 16):
                    stacked[k, u * (UNIT // 16) + g, :n_wide, :] = value[:, 128 * g : 128 * (g + 1)]
            if tasks:
                tasks.pop(0)()

    def wait_grads(s):
        grads = grad.at[s, pl.ds(0, (n_wide - 1) * depth), :]
        pltpu.make_async_copy(grads, grads, grad_recv_sem.at[s]).wait()

    def first_task():
        finish_wide(0)
        finish_tall(0)
        send_sibling(0)

    wait_grads(0)
    score_stage(0, [])
    for s in range(1, pieces):
        wait_grads(s)
    score_stage(1, [])
    score_stage(2, [first_task])
    rep_copy = score_send(1 - r, peer(0, 1, 0))

    @pl.when(r == 1)
    def _():
        rep_copy.start()

    score_stage(3, [])
    finish_wide(1)
    finish_tall(1)
    send_sibling(1)

    @pl.when(r == 0)
    def _():
        rep_copy.start()


    incoming[slot] = outgoing[r, c, z]

    @pl.when(r == c)
    def _():
        pltpu.make_async_copy(diag_bytes, diag_bytes, diag_sem.at[0]).wait()

    for copy in inner_copies:
        copy.wait_send()
    for s in range(pieces):
        grads = grad.at[s, pl.ds(0, (n_wide - 1) * depth), :]
        pltpu.make_async_copy(grads, grads, grad_send_sem.at[s]).wait()
    messages = incoming.at[pl.ds(0, 4 * n_wide - 1)]
    pltpu.make_async_copy(messages, messages, score_recv_sem).wait()
    pltpu.make_async_copy(messages, messages, score_send_sem).wait()
    out_ref[...] = jnp.sum(incoming[...], axis=0)


def fused_shards(
    n_wide, activations, deltas, act_factor, delta_factor, queries, assignment, padding
):
    _, tokens, features = activations.shape
    n_queries, rows, columns = queries.shape
    half = act_factor.shape[1]
    pieces = PIECES
    depth = rows // pieces
    block_size = n_queries // 4
    hbm = pl.BlockSpec(memory_space=pl.ANY)
    dma = pltpu.SemaphoreType.DMA
    bf16, f32 = jnp.bfloat16, jnp.float32
    return pl.pallas_call(
        functools.partial(kernel, n_wide, pieces),
        out_shape=pltpu.VMEM((1, block_size), f32),
        in_specs=[hbm] * 7,
        out_specs=pl.BlockSpec(memory_space=pltpu.VMEM),
        scratch_shapes=[
            pltpu.SMEM((n_wide,), jnp.int32),
            pltpu.SMEM((1,), jnp.int32),
            pltpu.VMEM((tokens, features), bf16),
            pltpu.VMEM((tokens, features), bf16),
            pltpu.VMEM((features, half), bf16),
            pltpu.VMEM((features, half), bf16),
            pltpu.VMEM((n_queries, rows, columns), bf16),
            pltpu.VMEM((half, half), bf16),
            pltpu.VMEM((pieces, n_wide * depth, features), f32),
            pltpu.VMEM((pieces, n_wide * depth, features), bf16),
            pltpu.VMEM((pieces, n_wide * depth, features), bf16),
            pltpu.VMEM((half, half), bf16),
            pltpu.VMEM((half, half), bf16),
            pltpu.VMEM((n_wide * depth, columns), f32),
            pltpu.VMEM((pieces, n_wide * depth, columns), bf16),
            pltpu.VMEM((n_wide, rows, columns), bf16),
            pltpu.VMEM((8 * n_wide, 8 * block_size), f32),
            pltpu.VMEM((2, block_size // 16, 8, 128), f32),
            pltpu.VMEM((2, block_size, 8 * n_wide), f32),
            pltpu.VMEM((2, 2, n_wide, 1, block_size), f32),
            pltpu.VMEM((4 * n_wide, 1, block_size), f32),
            pltpu.SemaphoreType.REGULAR((n_wide,)),
            dma((6,)),
            dma((10,)),
            dma((2,)),
            dma((pieces,)),
            dma((pieces,)),
            dma((pieces,)),
            dma((pieces,)),
            dma,
            dma,
        ],
        compiler_params=pltpu.CompilerParams(
            collective_id=0, has_side_effects=True, vmem_limit_bytes=60 * 1024 * 1024
        ),
    )(
        assignment,
        padding,
        activations.reshape(tokens, features),
        deltas.reshape(tokens, features),
        act_factor,
        delta_factor,
        queries,
    )


def solution(mesh):
    placed = (
        P(("parts", "wide"), "sub", None),
        P(("parts", "wide"), "sub", None),
        P(None, "rep"),
        P(None, "rep"),
        P(None, ("rep", "wide"), "sub"),
        P("parts"),
        P(("parts", "wide")),
    )
    n_wide, n_rep, n_sub = (mesh.shape[name] for name in ("wide", "rep", "sub"))

    def shards(activations, deltas, act_factor, delta_factor, queries, assignment, padding):
        seq_dev, tokens, features = activations.shape
        n_queries, rows, columns = queries.shape
        fits = (
            seq_dev == 1
            and (n_rep, n_sub) == (2, 2)
            and n_wide <= 8
            and rows % (8 * PIECES) == 0
            and columns % 128 == 0
            and act_factor.shape[1] == columns == n_wide * rows
            and tokens % 16 == 0
            and n_queries % (4 * UNIT) == 0
            and n_queries * rows * columns * 2 <= 44 * 2**20
        )
        run = functools.partial(fused_shards, n_wide) if fits else general_shards
        return run(activations, deltas, act_factor, delta_factor, queries, assignment, padding)

    return jax.shard_map(
        shards,
        mesh=mesh,
        in_specs=placed,
        out_specs=P(("parts", "wide"), ("rep", "sub")),
        check_vma=False,
    )
```

```python
import functools

import jax
import jax.numpy as jnp
from jax import lax
from jax.experimental import pallas as pl
from jax.experimental.pallas import tpu as pltpu
from jax.sharding import PartitionSpec as P

MESH = pl.DeviceIdType.MESH
UNIT = 32
PIECES = 2
EARLY = 2
SPLIT = 6
DIAG_PARTS = 1
LEAD = 4


def general_shards(
    activations, deltas, act_factor, delta_factor, queries, assignment, padding
):
    seq_dev, tok_dev, feature_width = activations.shape
    full_length = tok_dev * lax.axis_size("sub")
    token_start = lax.axis_index("sub") * tok_dev
    positions = token_start + lax.broadcasted_iota(jnp.int32, (seq_dev, tok_dev), 1)
    kept_mask = positions < (full_length - padding)[:, None]
    masked = jnp.where(kept_mask[:, :, None], deltas, jnp.zeros((), jnp.bfloat16))
    delta_proj = jnp.einsum(
        "stw,wi->sti", masked, delta_factor, preferred_element_type=jnp.float32
    ).astype(jnp.bfloat16)
    act_proj = jnp.einsum(
        "stw,wj->stj",
        activations,
        lax.all_gather(act_factor, "rep", axis=1, tiled=True),
        preferred_element_type=jnp.float32,
    ).astype(jnp.bfloat16)
    partial_value = jnp.einsum(
        "sti,stj->sij", delta_proj, act_proj, preferred_element_type=jnp.float32
    )
    summed = lax.psum_scatter(partial_value, "sub", scatter_dimension=2, tiled=True).astype(
        jnp.bfloat16
    )
    regrouped = lax.all_to_all(summed, "wide", split_axis=1, concat_axis=0, tiled=True)
    seq_total = regrouped.shape[0]
    grad_rows = regrouped.reshape(seq_total, -1)
    query_rows = queries.reshape(queries.shape[0], -1)
    partial_scores = lax.dot_general(
        grad_rows, query_rows, (((1,), (1,)), ((), ())), preferred_element_type=jnp.float32
    )
    inverse_order = (
        jnp.zeros((seq_total,), jnp.int32)
        .at[assignment]
        .set(jnp.arange(seq_total, dtype=jnp.int32))
    )
    ranked = jnp.take(partial_scores, inverse_order, axis=0)
    by_column = lax.psum_scatter(ranked, ("rep", "sub"), scatter_dimension=1, tiled=True)
    return lax.psum_scatter(by_column, "wide", scatter_dimension=0, tiled=True)


def kernel(
    n_wide,
    pieces,
    assignment_hbm,
    padding_hbm,
    act_hbm,
    delta_hbm,
    act_factor_hbm,
    delta_factor_hbm,
    query_hbm,
    out_ref,
    assignment,
    padding,
    act,
    delta,
    act_factor,
    delta_factor,
    query,
    diag,
    inner_mine,
    inner_sent,
    inner_theirs,
    factor_near,
    factor_far,
    grad_near,
    grad,
    grad_all,
    total_wide,
    stacked,
    tall_sums,
    outgoing,
    incoming,
    ready_sem,
    load_sem,
    query_sem,
    diag_sem,
    inner_send_sem,
    inner_recv_sem,
    grad_send_sem,
    grad_recv_sem,
    score_send_sem,
    score_recv_sem,
):
    z = lax.axis_index("wide")
    r = lax.axis_index("rep")
    c = lax.axis_index("sub")
    n_queries, rows, columns = query.shape
    depth = rows // pieces
    block_size = n_queries // 4
    pair = 2 * block_size
    f32, bf16 = jnp.float32, jnp.bfloat16

    def peer(dz, dr, dc):
        return {
            "wide": lax.rem(z + dz, n_wide),
            "rep": lax.rem(r + dr, 2),
            "sub": lax.rem(c + dc, 2),
        }

    def signal_wide(sem, place):
        pl.semaphore_signal(sem, inc=1, device_id={"wide": place}, device_id_type=MESH)

    barrier = pltpu.get_barrier_semaphore()
    for offset in ((0, 0, 1), (0, 1, 0)):
        pl.semaphore_signal(barrier, inc=1, device_id=peer(*offset), device_id_type=MESH)
    has_below, has_above = z > 0, z < n_wide - 1

    @pl.when(has_below)
    def _():
        signal_wide(barrier, z - 1)

    @pl.when(has_above)
    def _():
        signal_wide(barrier, z + 1)

    loads = [
        pltpu.make_async_copy(src, dst, load_sem.at[k])
        for k, (src, dst) in enumerate(
            (
                (act_factor_hbm, act_factor),
                (padding_hbm, padding),
                (delta_factor_hbm, delta_factor),
                (delta_hbm, delta),
                (act_hbm, act),
                (assignment_hbm, assignment),
            )
        )
    ]
    for load in loads:
        load.start()

    units = block_size // UNIT
    tiles = rows // 8
    cut = tiles // pieces
    stages = (
        ((0, 0, LEAD, 0, cut),),
        ((0, 0, LEAD, cut, tiles), (0, LEAD, units, 0, tiles)),
        ((1, 0, SPLIT, 0, tiles),),
        ((1, SPLIT, units, 0, tiles),),
    )
    query_slots = [(stage, part) for stage in stages for part in stage]

    def query_copies(stage):
        for part in stages[stage]:
            k, low, high, top, bottom = part
            place = query_slots.index((stages[stage], part))
            for side in (0, 1):
                first = k * pair + side * block_size + low * UNIT
                span = pl.ds(first, (high - low) * UNIT)
                lines = pl.ds(8 * top, 8 * (bottom - top))
                yield pltpu.make_async_copy(
                    query_hbm.at[span, lines, :],
                    query.at[span, lines, :],
                    query_sem.at[2 * place + side],
                )

    query_starts = [copy for stage in range(len(stages)) for copy in query_copies(stage)]
    for copy in query_starts[:EARLY]:
        copy.start()

    half = act_factor.shape[1]
    pl.semaphore_wait(barrier, 2 + has_below.astype(jnp.int32) + has_above.astype(jnp.int32))

    @pl.when(has_below & has_above)
    def _():
        signal_wide(ready_sem.at[z + 1], z - 1)
        signal_wide(ready_sem.at[z - 1], z + 1)

    quarter = half // 2
    piece_rows = quarter // DIAG_PARTS

    def diag_copy(k):
        width = quarter if k < DIAG_PARTS else half
        return pltpu.make_async_remote_copy(
            src_ref=act_factor.at[
                pl.ds(pl.multiple_of(c * half + k * piece_rows, piece_rows), piece_rows),
                pl.ds(0, width),
            ],
            dst_ref=diag.at[pl.ds(k * piece_rows, piece_rows), pl.ds(0, width)],
            send_sem=diag_sem.at[0],
            recv_sem=diag_sem.at[1],
            device_id=peer(0, 1, 0),
            device_id_type=MESH,
        )

    diag_bytes = diag.at[pl.ds(0, quarter + quarter // 2), :]

    loads[0].wait()

    @pl.when(r == c)
    def _():
        for k in range(2 * DIAG_PARTS):
            diag_copy(k).start()

    for load in loads[1:4]:
        load.wait()
    tokens = delta.shape[0]
    limit = 2 * tokens - padding[0] - c * tokens
    position = lax.broadcasted_iota(jnp.int32, (half, tokens), 1)
    projected = lax.dot_general(
        delta_factor[...], delta[...], (((0,), (1,)), ((), ())), preferred_element_type=f32
    )
    delta_proj = jnp.where(position < limit, projected, 0.0).astype(bf16)

    loads[4].wait()
    for copy in query_starts[EARLY:]:
        copy.start()
    inner = jnp.dot(delta_proj, act[...], preferred_element_type=f32)
    inner_copies = []
    for s in range(pieces):
        for p in range(n_wide):
            first = p * rows + s * depth
            part = inner[first : first + depth, :]
            inner_sent[s, p * depth : (p + 1) * depth, :] = part.astype(bf16)
            inner_mine[s, p * depth : (p + 1) * depth, :] = part
        copy = pltpu.make_async_remote_copy(
            src_ref=inner_sent.at[s],
            dst_ref=inner_theirs.at[s],
            send_sem=inner_send_sem.at[s],
            recv_sem=inner_recv_sem.at[s],
            device_id=peer(0, 0, 1),
            device_id_type=MESH,
        )
        copy.start()
        inner_copies.append(copy)

    stacked[...] = jnp.zeros(stacked.shape, f32)

    for d in range(2, n_wide):

        @pl.when((z + d < n_wide) & has_below)
        def _(d=d):
            pl.semaphore_wait(ready_sem.at[z + d], 1)
            signal_wide(ready_sem.at[z + d], z - 1)

        @pl.when((z - d >= 0) & has_above)
        def _(d=d):
            pl.semaphore_wait(ready_sem.at[z - d], 1)
            signal_wide(ready_sem.at[z - d], z + 1)

    near = pl.ds(pl.multiple_of(r * half, half), half)
    far = pl.ds(pl.multiple_of((1 - r) * half, half), half)

    @pl.when(r == c)
    def _():
        factor_near[...] = act_factor[near, :]
        factor_far[...] = act_factor[far, :]

    @pl.when(r != c)
    def _():
        factor_near[...] = act_factor[far, :].astype(f32).T.astype(bf16)

    def grad_copy(s, source, place):
        target = pl.ds(pl.multiple_of(place * depth, depth), depth)
        return pltpu.make_async_remote_copy(
            src_ref=grad.at[s, target, :],
            dst_ref=grad_all.at[source, pl.ds(s * depth, depth), :],
            send_sem=grad_send_sem.at[s],
            recv_sem=grad_recv_sem.at[s],
            device_id={"wide": place},
            device_id_type=MESH,
        )

    def others():
        for step in range(n_wide - 1):
            low = n_wide - 1 - step
            yield jnp.where(2 * z < n_wide, low - (low <= z), step + (step >= z))

    def product(s, lanes, factor):
        both = inner_mine[s, :, lanes] + inner_theirs[s, :, lanes].astype(f32)
        high = both.astype(bf16)
        low = (both - high.astype(f32)).astype(bf16)
        return jnp.dot(high, factor[...], preferred_element_type=f32) + jnp.dot(
            low, factor[...], preferred_element_type=f32
        )

    def wait_ends():
        @pl.when(z == 0)
        def _():
            for place in range(2, n_wide):
                pl.semaphore_wait(ready_sem.at[place], 1)

        @pl.when(z == n_wide - 1)
        def _():
            for place in range(n_wide - 2):
                pl.semaphore_wait(ready_sem.at[place], 1)

    inner_copies[0].wait_recv()
    grad_near[...] = product(0, near, factor_near)

    @pl.when(r != c)
    def _():
        pltpu.make_async_copy(diag_bytes, diag_bytes, diag_sem.at[1]).wait()
        factor_far[:, :quarter] = diag[:, :quarter]
        factor_far[quarter:, quarter:] = diag[quarter:, quarter:]
        factor_far[:quarter, quarter:] = diag[quarter:, :quarter].astype(f32).T.astype(bf16)

    for s in range(pieces):
        if s:
            inner_copies[s].wait_recv()
            grad_near[...] = product(s, near, factor_near)
        grad[s] = (grad_near[...] + product(s, far, factor_far)).astype(bf16)
        if s == 0:
            wait_ends()
        for place in others():
            grad_copy(s, z, place).start()
        own = pl.ds(pl.multiple_of(z * depth, depth), depth)
        grad_all[z, s * depth : (s + 1) * depth, :] = grad[s, own, :]

    loads[5].wait()
    stack = 8 * n_wide
    place_lane = lax.broadcasted_iota(jnp.int32, (8, stack), 1) // 8
    ranks = jnp.zeros((8, stack), jnp.int32)
    for n in range(n_wide):
        ranks = jnp.where(place_lane == n, assignment[n], ranks)
    rank_rows = lax.broadcasted_iota(jnp.int32, (8, stack), 0)
    places = jnp.where(ranks == rank_rows, 1.0, 0.0).astype(bf16)
    segments = block_size // 16
    gather = jnp.where(
        lax.broadcasted_iota(jnp.int32, (128, block_size), 0) // 8
        == lax.rem(lax.broadcasted_iota(jnp.int32, (128, block_size), 1), 16),
        1.0,
        0.0,
    ).astype(bf16)
    segment_of_lane = lax.broadcasted_iota(jnp.int32, (8, block_size), 1) // 16
    contract = (((1,), (1,)), ((), ()))

    def split(values):
        high = values.astype(bf16)
        return high, (values - high.astype(f32)).astype(bf16)

    def matches(shape, row_axis, lane_axis):
        return lax.rem(lax.broadcasted_iota(jnp.int32, shape, row_axis), 8) == lax.rem(
            lax.broadcasted_iota(jnp.int32, shape, lane_axis), 8
        )

    def weights(a):
        return grad_all[:, 8 * a : 8 * a + 8, :].reshape(stack, columns)

    def tile(start, a):
        span = pl.ds(pl.multiple_of(start, UNIT), UNIT)
        return query[span, 8 * a : 8 * a + 8, :].reshape(8 * UNIT, columns)

    def device_of(place):
        return (place["wide"] * 2 + place["rep"]) * 2 + place["sub"]

    slot = device_of(peer(0, 0, 0))

    def score_send(k, where):
        return pltpu.make_async_remote_copy(
            src_ref=outgoing.at[k, where["sub"], where["wide"]],
            dst_ref=incoming.at[slot],
            send_sem=score_send_sem,
            recv_sem=score_recv_sem,
            device_id=where,
            device_id_type=MESH,
        )

    def send_side(k, side):
        for dz in range(n_wide - 1, 0, -1):
            where = {"wide": lax.rem(z + dz, n_wide), "rep": k, "sub": side}
            score_send(k, where).start()

    def send_sibling(k):
        score_send(k, {"wide": z, "rep": k, "sub": 1 - c}).start()

    def send_all(k):
        send_side(k, 1)
        send_side(k, 0)
        send_sibling(k)

    def lanes_of(u):
        return slice(8 * UNIT * u, 8 * UNIT * (u + 1))

    def finish_wide(k):
        high, low = split(stacked[k].reshape(8 * segments, 128))
        spread = jnp.dot(high, gather, preferred_element_type=f32) + jnp.dot(
            low, gather, preferred_element_type=f32
        )
        scores = jnp.zeros((8, block_size), f32)
        for g in range(segments):
            scores = jnp.where(segment_of_lane == g, spread[8 * g : 8 * g + 8], scores)
        for p in range(n_wide):
            row = scores[0:1, :]
            for n in range(1, n_wide):
                row = jnp.where(assignment[n] == p, scores[n : n + 1, :], row)
            outgoing[k, 0, p] = row

    def finish_tall(k):
        high, low = split(tall_sums[k])
        scores = lax.dot_general(
            places, high, contract, preferred_element_type=f32
        ) + lax.dot_general(places, low, contract, preferred_element_type=f32)
        for p in range(n_wide):
            outgoing[k, 1, p] = scores[p : p + 1, :]

    def score_stage(stage, tasks):
        for copy in query_copies(stage):
            copy.wait()
        groups = [
            (part, first) for part in stages[stage] for first in range(part[1], part[2], 2)
        ]
        for (k, low, high, top, bottom), first in groups:
            base = k * pair
            group = range(first, min(high, first + 2))
            wide, tall = {}, {}
            for a in range(top, bottom):
                for u in group:
                    term = lax.dot_general(
                        weights(a), tile(base + u * UNIT, a), contract, preferred_element_type=f32
                    )
                    wide[u] = wide[u] + term if u in wide else term
                for u in group:
                    term = lax.dot_general(
                        tile(base + block_size + u * UNIT, a),
                        weights(a),
                        contract,
                        preferred_element_type=f32,
                    )
                    tall[u] = tall[u] + term if u in tall else term
            for u in group:
                span = slice(UNIT * u, UNIT * (u + 1))
                value = jnp.where(matches(tall[u].shape, 0, 1), tall[u], 0.0)
                summed = jnp.sum(value.reshape(UNIT, 8, stack), axis=1)
                tall_sums[k, span, :] = tall_sums[k, span, :] + summed if top else summed
                value = jnp.where(matches(wide[u].shape, 0, 1), wide[u], 0.0)
                if top:
                    value = value + total_wide[:, lanes_of(u)]
                if bottom < tiles:
                    total_wide[:, lanes_of(u)] = value
                    continue
                value = jnp.sum(value.reshape(n_wide, 8, 8 * UNIT), axis=1)
                for g in range(UNIT // 16):
                    stacked[k, u * (UNIT // 16) + g, :n_wide, :] = value[:, 128 * g : 128 * (g + 1)]
            if tasks:
                tasks.pop(0)()

    def wait_grads(s):
        grads = grad.at[s, pl.ds(0, (n_wide - 1) * depth), :]
        pltpu.make_async_copy(grads, grads, grad_recv_sem.at[s]).wait()

    def first_task():
        finish_tall(0)
        finish_wide(0)
        send_all(0)

    wait_grads(0)
    score_stage(0, [])
    for s in range(1, pieces):
        wait_grads(s)
    score_stage(1, [])
    score_stage(2, [first_task])
    rep_copy = score_send(1 - r, peer(0, 1, 0))

    @pl.when(r == 1)
    def _():
        rep_copy.start()

    score_stage(3, [])
    finish_tall(1)
    finish_wide(1)
    send_all(1)

    @pl.when(r == 0)
    def _():
        rep_copy.start()


    incoming[slot] = outgoing[r, c, z]

    @pl.when(r == c)
    def _():
        pltpu.make_async_copy(diag_bytes, diag_bytes, diag_sem.at[0]).wait()

    for copy in inner_copies:
        copy.wait_send()
    for s in range(pieces):
        grads = grad.at[s, pl.ds(0, (n_wide - 1) * depth), :]
        pltpu.make_async_copy(grads, grads, grad_send_sem.at[s]).wait()
    messages = incoming.at[pl.ds(0, 4 * n_wide - 1)]
    pltpu.make_async_copy(messages, messages, score_recv_sem).wait()
    out_ref[...] = jnp.sum(incoming[...], axis=0)
    pltpu.make_async_copy(messages, messages, score_send_sem).wait()


def fused_shards(
    n_wide, activations, deltas, act_factor, delta_factor, queries, assignment, padding
):
    _, tokens, features = activations.shape
    n_queries, rows, columns = queries.shape
    half = act_factor.shape[1]
    pieces = PIECES
    depth = rows // pieces
    block_size = n_queries // 4
    hbm = pl.BlockSpec(memory_space=pl.ANY)
    dma = pltpu.SemaphoreType.DMA
    bf16, f32 = jnp.bfloat16, jnp.float32
    return pl.pallas_call(
        functools.partial(kernel, n_wide, pieces),
        out_shape=pltpu.VMEM((1, block_size), f32),
        in_specs=[hbm] * 7,
        out_specs=pl.BlockSpec(memory_space=pltpu.VMEM),
        scratch_shapes=[
            pltpu.SMEM((n_wide,), jnp.int32),
            pltpu.SMEM((1,), jnp.int32),
            pltpu.VMEM((tokens, features), bf16),
            pltpu.VMEM((tokens, features), bf16),
            pltpu.VMEM((features, half), bf16),
            pltpu.VMEM((features, half), bf16),
            pltpu.VMEM((n_queries, rows, columns), bf16),
            pltpu.VMEM((half, half), bf16),
            pltpu.VMEM((pieces, n_wide * depth, features), f32),
            pltpu.VMEM((pieces, n_wide * depth, features), bf16),
            pltpu.VMEM((pieces, n_wide * depth, features), bf16),
            pltpu.VMEM((half, half), bf16),
            pltpu.VMEM((half, half), bf16),
            pltpu.VMEM((n_wide * depth, columns), f32),
            pltpu.VMEM((pieces, n_wide * depth, columns), bf16),
            pltpu.VMEM((n_wide, rows, columns), bf16),
            pltpu.VMEM((8 * n_wide, 8 * block_size), f32),
            pltpu.VMEM((2, block_size // 16, 8, 128), f32),
            pltpu.VMEM((2, block_size, 8 * n_wide), f32),
            pltpu.VMEM((2, 2, n_wide, 1, block_size), f32),
            pltpu.VMEM((4 * n_wide, 1, block_size), f32),
            pltpu.SemaphoreType.REGULAR((n_wide,)),
            dma((6,)),
            dma((10,)),
            dma((2,)),
            dma((pieces,)),
            dma((pieces,)),
            dma((pieces,)),
            dma((pieces,)),
            dma,
            dma,
        ],
        compiler_params=pltpu.CompilerParams(
            collective_id=0, has_side_effects=True, vmem_limit_bytes=60 * 1024 * 1024
        ),
    )(
        assignment,
        padding,
        activations.reshape(tokens, features),
        deltas.reshape(tokens, features),
        act_factor,
        delta_factor,
        queries,
    )


def solution(mesh):
    placed = (
        P(("parts", "wide"), "sub", None),
        P(("parts", "wide"), "sub", None),
        P(None, "rep"),
        P(None, "rep"),
        P(None, ("rep", "wide"), "sub"),
        P("parts"),
        P(("parts", "wide")),
    )
    n_wide, n_rep, n_sub = (mesh.shape[name] for name in ("wide", "rep", "sub"))

    def shards(activations, deltas, act_factor, delta_factor, queries, assignment, padding):
        seq_dev, tokens, features = activations.shape
        n_queries, rows, columns = queries.shape
        fits = (
            seq_dev == 1
            and (n_rep, n_sub) == (2, 2)
            and n_wide <= 8
            and rows % (8 * PIECES) == 0
            and columns % 128 == 0
            and act_factor.shape[1] == columns == n_wide * rows
            and tokens % 16 == 0
            and n_queries % (4 * UNIT) == 0
            and n_queries * rows * columns * 2 <= 44 * 2**20
        )
        run = functools.partial(fused_shards, n_wide) if fits else general_shards
        return run(activations, deltas, act_factor, delta_factor, queries, assignment, padding)

    return jax.shard_map(
        shards,
        mesh=mesh,
        in_specs=placed,
        out_specs=P(("parts", "wide"), ("rep", "sub")),
        check_vma=False,
    )
```

```python
import functools

import jax
import jax.numpy as jnp
from jax import lax
from jax.experimental import pallas as pl
from jax.experimental.pallas import tpu as pltpu
from jax.sharding import PartitionSpec as P

MESH = pl.DeviceIdType.MESH
UNIT = 32
PIECES = 2
EARLY = 2
SPLIT = 6
DIAG_PARTS = 1
LEAD = 4


def general_shards(
    activations, deltas, act_factor, delta_factor, queries, assignment, padding
):
    seq_dev, tok_dev, feature_width = activations.shape
    full_length = tok_dev * lax.axis_size("sub")
    token_start = lax.axis_index("sub") * tok_dev
    positions = token_start + lax.broadcasted_iota(jnp.int32, (seq_dev, tok_dev), 1)
    kept_mask = positions < (full_length - padding)[:, None]
    masked = jnp.where(kept_mask[:, :, None], deltas, jnp.zeros((), jnp.bfloat16))
    delta_proj = jnp.einsum(
        "stw,wi->sti", masked, delta_factor, preferred_element_type=jnp.float32
    ).astype(jnp.bfloat16)
    act_proj = jnp.einsum(
        "stw,wj->stj",
        activations,
        lax.all_gather(act_factor, "rep", axis=1, tiled=True),
        preferred_element_type=jnp.float32,
    ).astype(jnp.bfloat16)
    partial_value = jnp.einsum(
        "sti,stj->sij", delta_proj, act_proj, preferred_element_type=jnp.float32
    )
    summed = lax.psum_scatter(partial_value, "sub", scatter_dimension=2, tiled=True).astype(
        jnp.bfloat16
    )
    regrouped = lax.all_to_all(summed, "wide", split_axis=1, concat_axis=0, tiled=True)
    seq_total = regrouped.shape[0]
    grad_rows = regrouped.reshape(seq_total, -1)
    query_rows = queries.reshape(queries.shape[0], -1)
    partial_scores = lax.dot_general(
        grad_rows, query_rows, (((1,), (1,)), ((), ())), preferred_element_type=jnp.float32
    )
    inverse_order = (
        jnp.zeros((seq_total,), jnp.int32)
        .at[assignment]
        .set(jnp.arange(seq_total, dtype=jnp.int32))
    )
    ranked = jnp.take(partial_scores, inverse_order, axis=0)
    by_column = lax.psum_scatter(ranked, ("rep", "sub"), scatter_dimension=1, tiled=True)
    return lax.psum_scatter(by_column, "wide", scatter_dimension=0, tiled=True)


def kernel(
    n_wide,
    pieces,
    assignment_hbm,
    padding_hbm,
    act_hbm,
    delta_hbm,
    act_factor_hbm,
    delta_factor_hbm,
    query_hbm,
    out_ref,
    assignment,
    padding,
    act,
    delta,
    act_factor,
    delta_factor,
    query,
    diag,
    inner_mine,
    inner_sent,
    inner_theirs,
    factor_near,
    factor_far,
    grad_near,
    grad,
    grad_all,
    total_wide,
    stacked,
    tall_sums,
    outgoing,
    incoming,
    ready_sem,
    load_sem,
    query_sem,
    diag_sem,
    inner_send_sem,
    inner_recv_sem,
    grad_send_sem,
    grad_recv_sem,
    score_send_sem,
    score_recv_sem,
):
    z = lax.axis_index("wide")
    r = lax.axis_index("rep")
    c = lax.axis_index("sub")
    n_queries, rows, columns = query.shape
    depth = rows // pieces
    block_size = n_queries // 4
    pair = 2 * block_size
    f32, bf16 = jnp.float32, jnp.bfloat16

    def peer(dz, dr, dc):
        return {
            "wide": lax.rem(z + dz, n_wide),
            "rep": lax.rem(r + dr, 2),
            "sub": lax.rem(c + dc, 2),
        }

    def signal_wide(sem, place):
        pl.semaphore_signal(sem, inc=1, device_id={"wide": place}, device_id_type=MESH)

    barrier = pltpu.get_barrier_semaphore()
    for offset in ((0, 0, 1), (0, 1, 0)):
        pl.semaphore_signal(barrier, inc=1, device_id=peer(*offset), device_id_type=MESH)
    has_below, has_above = z > 0, z < n_wide - 1

    @pl.when(has_below)
    def _():
        signal_wide(barrier, z - 1)

    @pl.when(has_above)
    def _():
        signal_wide(barrier, z + 1)

    loads = [
        pltpu.make_async_copy(src, dst, load_sem.at[k])
        for k, (src, dst) in enumerate(
            (
                (act_factor_hbm, act_factor),
                (padding_hbm, padding),
                (delta_factor_hbm, delta_factor),
                (delta_hbm, delta),
                (act_hbm, act),
                (assignment_hbm, assignment),
            )
        )
    ]
    for load in loads:
        load.start()

    units = block_size // UNIT
    tiles = rows // 8
    cut = tiles // pieces
    stages = (
        ((0, 0, LEAD, 0, cut),),
        ((0, 0, LEAD, cut, tiles), (0, LEAD, units, 0, tiles)),
        ((1, 0, SPLIT, 0, tiles),),
        ((1, SPLIT, units, 0, tiles),),
    )
    query_slots = [(stage, part) for stage in stages for part in stage]

    def query_copies(stage):
        for part in stages[stage]:
            k, low, high, top, bottom = part
            place = query_slots.index((stages[stage], part))
            for side in (0, 1):
                first = k * pair + side * block_size + low * UNIT
                span = pl.ds(first, (high - low) * UNIT)
                lines = pl.ds(8 * top, 8 * (bottom - top))
                yield pltpu.make_async_copy(
                    query_hbm.at[span, lines, :],
                    query.at[span, lines, :],
                    query_sem.at[2 * place + side],
                )

    query_starts = [copy for stage in range(len(stages)) for copy in query_copies(stage)]
    for copy in query_starts[:EARLY]:
        copy.start()

    half = act_factor.shape[1]
    pl.semaphore_wait(barrier, 2 + has_below.astype(jnp.int32) + has_above.astype(jnp.int32))

    @pl.when(has_below & has_above)
    def _():
        signal_wide(ready_sem.at[z + 1], z - 1)
        signal_wide(ready_sem.at[z - 1], z + 1)

    quarter = half // 2
    piece_rows = quarter // DIAG_PARTS

    def diag_copy(k):
        width = quarter if k < DIAG_PARTS else half
        return pltpu.make_async_remote_copy(
            src_ref=act_factor.at[
                pl.ds(pl.multiple_of(c * half + k * piece_rows, piece_rows), piece_rows),
                pl.ds(0, width),
            ],
            dst_ref=diag.at[pl.ds(k * piece_rows, piece_rows), pl.ds(0, width)],
            send_sem=diag_sem.at[0],
            recv_sem=diag_sem.at[1],
            device_id=peer(0, 1, 0),
            device_id_type=MESH,
        )

    diag_bytes = diag.at[pl.ds(0, quarter + quarter // 2), :]

    loads[0].wait()

    @pl.when(r == c)
    def _():
        for k in range(2 * DIAG_PARTS):
            diag_copy(k).start()

    for load in loads[1:4]:
        load.wait()
    tokens = delta.shape[0]
    limit = 2 * tokens - padding[0] - c * tokens
    position = lax.broadcasted_iota(jnp.int32, (half, tokens), 1)
    projected = lax.dot_general(
        delta_factor[...], delta[...], (((0,), (1,)), ((), ())), preferred_element_type=f32
    )
    delta_proj = jnp.where(position < limit, projected, 0.0).astype(bf16)

    loads[4].wait()
    for copy in query_starts[EARLY:]:
        copy.start()
    inner = jnp.dot(delta_proj, act[...], preferred_element_type=f32)
    inner_copies = []
    for s in range(pieces):
        for p in range(n_wide):
            first = p * rows + s * depth
            part = inner[first : first + depth, :]
            inner_sent[s, p * depth : (p + 1) * depth, :] = part.astype(bf16)
            inner_mine[s, p * depth : (p + 1) * depth, :] = part
        copy = pltpu.make_async_remote_copy(
            src_ref=inner_sent.at[s],
            dst_ref=inner_theirs.at[s],
            send_sem=inner_send_sem.at[s],
            recv_sem=inner_recv_sem.at[s],
            device_id=peer(0, 0, 1),
            device_id_type=MESH,
        )
        copy.start()
        inner_copies.append(copy)

    stacked[...] = jnp.zeros(stacked.shape, f32)

    for d in range(2, n_wide):

        @pl.when((z + d < n_wide) & has_below)
        def _(d=d):
            pl.semaphore_wait(ready_sem.at[z + d], 1)
            signal_wide(ready_sem.at[z + d], z - 1)

        @pl.when((z - d >= 0) & has_above)
        def _(d=d):
            pl.semaphore_wait(ready_sem.at[z - d], 1)
            signal_wide(ready_sem.at[z - d], z + 1)

    near = pl.ds(pl.multiple_of(r * half, half), half)
    far = pl.ds(pl.multiple_of((1 - r) * half, half), half)

    @pl.when(r == c)
    def _():
        factor_near[...] = act_factor[near, :]
        factor_far[...] = act_factor[far, :]

    @pl.when(r != c)
    def _():
        factor_near[...] = act_factor[far, :].astype(f32).T.astype(bf16)

    def grad_copy(s, source, place):
        target = pl.ds(pl.multiple_of(place * depth, depth), depth)
        return pltpu.make_async_remote_copy(
            src_ref=grad.at[s, target, :],
            dst_ref=grad_all.at[source, pl.ds(s * depth, depth), :],
            send_sem=grad_send_sem.at[s],
            recv_sem=grad_recv_sem.at[s],
            device_id={"wide": place},
            device_id_type=MESH,
        )

    def others():
        for step in range(n_wide - 1):
            low = n_wide - 1 - step
            yield jnp.where(2 * z < n_wide, low - (low <= z), step + (step >= z))

    def product(s, lanes, factor):
        both = inner_mine[s, :, lanes] + inner_theirs[s, :, lanes].astype(f32)
        high = both.astype(bf16)
        low = (both - high.astype(f32)).astype(bf16)
        return jnp.dot(high, factor[...], preferred_element_type=f32) + jnp.dot(
            low, factor[...], preferred_element_type=f32
        )

    def wait_ends():
        @pl.when(z == 0)
        def _():
            for place in range(2, n_wide):
                pl.semaphore_wait(ready_sem.at[place], 1)

        @pl.when(z == n_wide - 1)
        def _():
            for place in range(n_wide - 2):
                pl.semaphore_wait(ready_sem.at[place], 1)

    inner_copies[0].wait_recv()
    grad_near[...] = product(0, near, factor_near)

    @pl.when(r != c)
    def _():
        pltpu.make_async_copy(diag_bytes, diag_bytes, diag_sem.at[1]).wait()
        factor_far[:, :quarter] = diag[:, :quarter]
        factor_far[quarter:, quarter:] = diag[quarter:, quarter:]
        factor_far[:quarter, quarter:] = diag[quarter:, :quarter].astype(f32).T.astype(bf16)

    for s in range(pieces):
        if s:
            inner_copies[s].wait_recv()
            grad_near[...] = product(s, near, factor_near)
        grad[s] = (grad_near[...] + product(s, far, factor_far)).astype(bf16)
        if s == 0:
            wait_ends()
        for place in others():
            grad_copy(s, z, place).start()
        own = pl.ds(pl.multiple_of(z * depth, depth), depth)
        grad_all[z, s * depth : (s + 1) * depth, :] = grad[s, own, :]

    loads[5].wait()
    stack = 8 * n_wide
    place_lane = lax.broadcasted_iota(jnp.int32, (8, stack), 1) // 8
    ranks = jnp.zeros((8, stack), jnp.int32)
    for n in range(n_wide):
        ranks = jnp.where(place_lane == n, assignment[n], ranks)
    rank_rows = lax.broadcasted_iota(jnp.int32, (8, stack), 0)
    places = jnp.where(ranks == rank_rows, 1.0, 0.0).astype(bf16)
    segments = block_size // 16
    gather = jnp.where(
        lax.broadcasted_iota(jnp.int32, (128, block_size), 0) // 8
        == lax.rem(lax.broadcasted_iota(jnp.int32, (128, block_size), 1), 16),
        1.0,
        0.0,
    ).astype(bf16)
    segment_of_lane = lax.broadcasted_iota(jnp.int32, (8, block_size), 1) // 16
    contract = (((1,), (1,)), ((), ()))

    def split(values):
        high = values.astype(bf16)
        return high, (values - high.astype(f32)).astype(bf16)

    def matches(shape, row_axis, lane_axis):
        return lax.rem(lax.broadcasted_iota(jnp.int32, shape, row_axis), 8) == lax.rem(
            lax.broadcasted_iota(jnp.int32, shape, lane_axis), 8
        )

    def weights(a):
        return grad_all[:, 8 * a : 8 * a + 8, :].reshape(stack, columns)

    def tile(start, a):
        span = pl.ds(pl.multiple_of(start, UNIT), UNIT)
        return query[span, 8 * a : 8 * a + 8, :].reshape(8 * UNIT, columns)

    def device_of(place):
        return (place["wide"] * 2 + place["rep"]) * 2 + place["sub"]

    slot = device_of(peer(0, 0, 0))

    def score_send(k, where):
        return pltpu.make_async_remote_copy(
            src_ref=outgoing.at[k, where["sub"], where["wide"]],
            dst_ref=incoming.at[slot],
            send_sem=score_send_sem,
            recv_sem=score_recv_sem,
            device_id=where,
            device_id_type=MESH,
        )

    def send_side(k, side):
        for place in others():
            score_send(k, {"wide": place, "rep": k, "sub": side}).start()

    def send_sibling(k):
        score_send(k, {"wide": z, "rep": k, "sub": 1 - c}).start()

    def send_all(k):
        send_side(k, 1)
        send_side(k, 0)
        send_sibling(k)

    def lanes_of(u):
        return slice(8 * UNIT * u, 8 * UNIT * (u + 1))

    def finish_wide(k):
        high, low = split(stacked[k].reshape(8 * segments, 128))
        spread = jnp.dot(high, gather, preferred_element_type=f32) + jnp.dot(
            low, gather, preferred_element_type=f32
        )
        scores = jnp.zeros((8, block_size), f32)
        for g in range(segments):
            scores = jnp.where(segment_of_lane == g, spread[8 * g : 8 * g + 8], scores)
        for p in range(n_wide):
            row = scores[0:1, :]
            for n in range(1, n_wide):
                row = jnp.where(assignment[n] == p, scores[n : n + 1, :], row)
            outgoing[k, 0, p] = row

    def finish_tall(k):
        high, low = split(tall_sums[k])
        scores = lax.dot_general(
            places, high, contract, preferred_element_type=f32
        ) + lax.dot_general(places, low, contract, preferred_element_type=f32)
        for p in range(n_wide):
            outgoing[k, 1, p] = scores[p : p + 1, :]

    def score_stage(stage, tasks):
        for copy in query_copies(stage):
            copy.wait()
        groups = [
            (part, first) for part in stages[stage] for first in range(part[1], part[2], 2)
        ]
        for (k, low, high, top, bottom), first in groups:
            base = k * pair
            group = range(first, min(high, first + 2))
            wide, tall = {}, {}
            for a in range(top, bottom):
                for u in group:
                    term = lax.dot_general(
                        weights(a), tile(base + u * UNIT, a), contract, preferred_element_type=f32
                    )
                    wide[u] = wide[u] + term if u in wide else term
                for u in group:
                    term = lax.dot_general(
                        tile(base + block_size + u * UNIT, a),
                        weights(a),
                        contract,
                        preferred_element_type=f32,
                    )
                    tall[u] = tall[u] + term if u in tall else term
            for u in group:
                span = slice(UNIT * u, UNIT * (u + 1))
                value = jnp.where(matches(tall[u].shape, 0, 1), tall[u], 0.0)
                summed = jnp.sum(value.reshape(UNIT, 8, stack), axis=1)
                tall_sums[k, span, :] = tall_sums[k, span, :] + summed if top else summed
                value = jnp.where(matches(wide[u].shape, 0, 1), wide[u], 0.0)
                if top:
                    value = value + total_wide[:, lanes_of(u)]
                if bottom < tiles:
                    total_wide[:, lanes_of(u)] = value
                    continue
                value = jnp.sum(value.reshape(n_wide, 8, 8 * UNIT), axis=1)
                for g in range(UNIT // 16):
                    stacked[k, u * (UNIT // 16) + g, :n_wide, :] = value[:, 128 * g : 128 * (g + 1)]
            if tasks:
                tasks.pop(0)()

    def wait_grads(s):
        grads = grad.at[s, pl.ds(0, (n_wide - 1) * depth), :]
        pltpu.make_async_copy(grads, grads, grad_recv_sem.at[s]).wait()

    def first_task():
        finish_tall(0)
        finish_wide(0)
        send_all(0)

    wait_grads(0)
    score_stage(0, [])
    for s in range(1, pieces):
        wait_grads(s)
    score_stage(1, [])
    score_stage(2, [first_task])
    rep_copy = score_send(1 - r, peer(0, 1, 0))

    @pl.when(r == 1)
    def _():
        rep_copy.start()

    score_stage(3, [])
    finish_tall(1)
    finish_wide(1)
    send_all(1)

    @pl.when(r == 0)
    def _():
        rep_copy.start()


    incoming[slot] = outgoing[r, c, z]

    @pl.when(r == c)
    def _():
        pltpu.make_async_copy(diag_bytes, diag_bytes, diag_sem.at[0]).wait()

    for copy in inner_copies:
        copy.wait_send()
    for s in range(pieces):
        grads = grad.at[s, pl.ds(0, (n_wide - 1) * depth), :]
        pltpu.make_async_copy(grads, grads, grad_send_sem.at[s]).wait()
    messages = incoming.at[pl.ds(0, 4 * n_wide - 1)]
    pltpu.make_async_copy(messages, messages, score_recv_sem).wait()
    out_ref[...] = jnp.sum(incoming[...], axis=0)
    pltpu.make_async_copy(messages, messages, score_send_sem).wait()


def fused_shards(
    n_wide, activations, deltas, act_factor, delta_factor, queries, assignment, padding
):
    _, tokens, features = activations.shape
    n_queries, rows, columns = queries.shape
    half = act_factor.shape[1]
    pieces = PIECES
    depth = rows // pieces
    block_size = n_queries // 4
    hbm = pl.BlockSpec(memory_space=pl.ANY)
    dma = pltpu.SemaphoreType.DMA
    bf16, f32 = jnp.bfloat16, jnp.float32
    return pl.pallas_call(
        functools.partial(kernel, n_wide, pieces),
        out_shape=pltpu.VMEM((1, block_size), f32),
        in_specs=[hbm] * 7,
        out_specs=pl.BlockSpec(memory_space=pltpu.VMEM),
        scratch_shapes=[
            pltpu.SMEM((n_wide,), jnp.int32),
            pltpu.SMEM((1,), jnp.int32),
            pltpu.VMEM((tokens, features), bf16),
            pltpu.VMEM((tokens, features), bf16),
            pltpu.VMEM((features, half), bf16),
            pltpu.VMEM((features, half), bf16),
            pltpu.VMEM((n_queries, rows, columns), bf16),
            pltpu.VMEM((half, half), bf16),
            pltpu.VMEM((pieces, n_wide * depth, features), f32),
            pltpu.VMEM((pieces, n_wide * depth, features), bf16),
            pltpu.VMEM((pieces, n_wide * depth, features), bf16),
            pltpu.VMEM((half, half), bf16),
            pltpu.VMEM((half, half), bf16),
            pltpu.VMEM((n_wide * depth, columns), f32),
            pltpu.VMEM((pieces, n_wide * depth, columns), bf16),
            pltpu.VMEM((n_wide, rows, columns), bf16),
            pltpu.VMEM((8 * n_wide, 8 * block_size), f32),
            pltpu.VMEM((2, block_size // 16, 8, 128), f32),
            pltpu.VMEM((2, block_size, 8 * n_wide), f32),
            pltpu.VMEM((2, 2, n_wide, 1, block_size), f32),
            pltpu.VMEM((4 * n_wide, 1, block_size), f32),
            pltpu.SemaphoreType.REGULAR((n_wide,)),
            dma((6,)),
            dma((10,)),
            dma((2,)),
            dma((pieces,)),
            dma((pieces,)),
            dma((pieces,)),
            dma((pieces,)),
            dma,
            dma,
        ],
        compiler_params=pltpu.CompilerParams(
            collective_id=0, has_side_effects=True, vmem_limit_bytes=60 * 1024 * 1024
        ),
    )(
        assignment,
        padding,
        activations.reshape(tokens, features),
        deltas.reshape(tokens, features),
        act_factor,
        delta_factor,
        queries,
    )


def solution(mesh):
    placed = (
        P(("parts", "wide"), "sub", None),
        P(("parts", "wide"), "sub", None),
        P(None, "rep"),
        P(None, "rep"),
        P(None, ("rep", "wide"), "sub"),
        P("parts"),
        P(("parts", "wide")),
    )
    n_wide, n_rep, n_sub = (mesh.shape[name] for name in ("wide", "rep", "sub"))

    def shards(activations, deltas, act_factor, delta_factor, queries, assignment, padding):
        seq_dev, tokens, features = activations.shape
        n_queries, rows, columns = queries.shape
        fits = (
            seq_dev == 1
            and (n_rep, n_sub) == (2, 2)
            and n_wide <= 8
            and rows % (8 * PIECES) == 0
            and columns % 128 == 0
            and act_factor.shape[1] == columns == n_wide * rows
            and tokens % 16 == 0
            and n_queries % (4 * UNIT) == 0
            and n_queries * rows * columns * 2 <= 44 * 2**20
        )
        run = functools.partial(fused_shards, n_wide) if fits else general_shards
        return run(activations, deltas, act_factor, delta_factor, queries, assignment, padding)

    return jax.shard_map(
        shards,
        mesh=mesh,
        in_specs=placed,
        out_specs=P(("parts", "wide"), ("rep", "sub")),
        check_vma=False,
    )
```
